32 devices in a mesh: ctx: 8 (over y, x, core), page: 4 (over z).
Axes of the slice: x: 2, y: 2, z: 4, core: 2. Of those that a mesh axis runs over, the one named last changes fastest.
Arguments:
- queries: bfloat16 [2048, 8192], P('ctx', 'page'), may hold values from -200 to 200
- keys: bfloat16 [2048, 512], P('ctx', 'page'), may hold values from -6 to 6
- values: bfloat16 [2048, 512], P('ctx', 'page'), may hold values from -6 to 6
- span_table: int32 [16], replicated, may hold values from 0 to 15, each once
- page_slots: int32 [16], replicated, may hold values from 0 to 15, each once
Outputs:
- attended: bfloat16 [2048, 8192], P('ctx', 'page')
- cache_pages: bfloat16 [16, 4, 2, 128, 128], P('ctx')
- cache_scales: float32 [16, 4, 2], P('ctx')
The draws below stay inside these ranges and needn't reach their ends.
Inputs may be any that keep to these rules, and one draw needn't show every extreme that they name: Stored span i (rows i * 128 to (i + 1) * 128 - 1) holds prompt positions span_table[i] * 128 onward; every value appears once. `page_slots`: every slot is named by exactly one page.
All inputs are finite; a program needn't handle non-finite values. Where the reference program divides by a largest or mean magnitude, that divisor is 1e-20 or more.
Results may differ from the reference program's by a relative error of at most 0.0055.
Values may be sent and summed in bfloat16 or wider, within the bound.
A program may use at most 64 MiB of HBM per device.

```python
import jax
import jax.numpy as jnp
from jax import lax

HQ = 64
KVH = 4
DH = 128
PAGE = 128
SPAN = 128
TOKENS = 2048
SLOTS = 16
N_CTX = 8


def common_draw(key):
    key_rows = jax.random.truncated_normal(jax.random.fold_in(key, 11), -6.0, 6.0, (TOKENS, KVH * DH), jnp.float32)
    query_rows = jax.random.truncated_normal(jax.random.fold_in(key, 12), -6.0, 6.0, (TOKENS, HQ * DH), jnp.float32)
    return (query_rows, key_rows)


def draw_queries(key, part):
    return common_draw(key)[0].astype(jnp.bfloat16)


def draw_keys(key, part):
    return common_draw(key)[1].astype(jnp.bfloat16)


def level_of(stream_key, shape, pieces, smallest, high):
    gain, own = 1.0, jax.random.fold_in(stream_key, 6)
    for dim, blocks in pieces:
        draws = jnp.exp(jax.random.uniform(jax.random.fold_in(own, dim), (blocks,), jnp.float32, smallest / len(pieces), high / len(pieces)))
        gain = gain * jnp.repeat(draws, shape[dim] // blocks).reshape([-1 if axis == dim else 1 for axis in range(len(shape))])
    return gain


def gaussian(rng, shape, scale, limit, shards=(), kind=jnp.bfloat16):
    level = level_of(rng, shape, shards, -0.22, 0.18) if shards else 1.0
    values = jax.random.normal(rng, shape, jnp.float32) * scale * level
    return jnp.minimum(jnp.maximum(values, -limit), limit).astype(kind)


def setup_inputs(seed: int = 0) -> dict:
    splits = jax.random.split(jax.random.key(seed), 6)
    return {
        "queries": draw_queries(jax.random.fold_in(splits[5], 71), 0),
        "keys": draw_keys(jax.random.fold_in(splits[5], 71), 0),
        "values": gaussian(splits[2], (TOKENS, KVH * DH), 1.0, 6.0, ((0, 8), (1, 4))),
        "span_table": jax.random.permutation(splits[3], 2 * N_CTX).astype(jnp.int32),
        "page_slots": jax.random.permutation(splits[4], SLOTS).astype(jnp.int32),
    }


def reference(queries, keys, values, span_table, page_slots):
    rows = jnp.arange(TOKENS, dtype=jnp.int32)
    pos = span_table[rows // SPAN] * SPAN + rows % SPAN
    group = HQ // KVH
    key_heads = keys.reshape(TOKENS, KVH, DH).astype(jnp.float32)
    value_heads = values.reshape(TOKENS, KVH, DH).astype(jnp.float32)
    scale = DH ** -0.5

    def block(index):
        start = (index * SPAN).astype(jnp.int32)
        query_block = lax.dynamic_slice_in_dim(queries, start, SPAN, 0)
        query_block = query_block.reshape(SPAN, KVH, group, DH).astype(jnp.float32)
        query_pos = lax.dynamic_slice_in_dim(pos, start, SPAN, 0)
        score = jnp.einsum('qhgd,khd->hgqk', query_block, key_heads) * scale
        keep = pos[None, :] <= query_pos[:, None]
        score = jnp.where(keep[None, None], score, -1e30)
        top = jnp.max(score, axis=-1, keepdims=True)
        weight = jnp.where(keep[None, None], jnp.exp(score - top), 0.0)
        total = jnp.sum(weight, axis=-1)
        weight_b = weight.astype(jnp.bfloat16).astype(jnp.float32)
        summed = jnp.einsum('hgqk,khd->qhgd', weight_b, value_heads)
        result = summed / jnp.transpose(total, (2, 0, 1))[..., None]
        return result.reshape(SPAN, HQ * DH).astype(jnp.bfloat16)

    attended = lax.map(block, jnp.arange(TOKENS // SPAN, dtype=jnp.int32)).reshape(TOKENS, HQ * DH)
    key_pages = keys.reshape(SLOTS, PAGE, KVH, DH).transpose(0, 2, 1, 3)
    value_pages = values.reshape(SLOTS, PAGE, KVH, DH).transpose(0, 2, 1, 3)
    stacked = jnp.stack([key_pages, value_pages], axis=2)
    page_of_slot = jnp.zeros((SLOTS,), jnp.int32).at[page_slots].set(jnp.arange(SLOTS, dtype=jnp.int32))
    raw = stacked[page_of_slot].astype(jnp.float32)
    cache_scales = jnp.max(jnp.abs(raw), axis=(3, 4)) + 1e-6
    cache_pages = (raw / cache_scales[..., None, None]).astype(jnp.bfloat16)
    return attended, cache_pages, cache_scales
```

```python
import functools
import math

import jax
import jax.numpy as jnp
from jax import lax
from jax.experimental import pallas as pl
from jax.experimental.pallas import tpu as pltpu
from jax.sharding import PartitionSpec as P

DH = 128
PAGE = 128
SPAN = 128
HIDE = -1e30
PAIR = 2
PIECES = (32, 32, 32, 32)
MESH = pl.DeviceIdType.MESH


def kernel(
    n, n_page, heads, spans, table_in, slots_in, q_in, k_in, v_in,
    att_out, cache_out, scales_out,
    table_ref, slots_ref, bias, own_bias, q_ref, own, qs, kc, vt, s0, s1, p0, p1,
    tops, acc, att, cache, scales, send, recv, own_sem, page_send, page_recv, out_sem,
    *pieces,
):
    count = len(PIECES)
    bufs, zbufs = pieces[:count], pieces[count:]
    starts = [sum(PIECES[:p]) for p in range(count)]
    chips = n // 2
    pairs = heads // PAIR
    wide = PAIR * SPAN
    units = pairs * spans
    me = lax.axis_index("ctx")
    page = lax.axis_index("page")
    chip = me // 2
    core = me % 2
    sibling = 2 * chip + 1 - core
    rate = DH ** (-0.5) * math.log2(math.e)

    def ahead(d):
        return 2 * ((chip + d) % chips) + core

    def behind(d, c):
        return 2 * ((chip + chips - d) % chips) + c

    barrier = pltpu.get_barrier_semaphore()
    for d in range(1, chips):
        pl.semaphore_signal(barrier, inc=1, device_id={"ctx": ahead(d)}, device_id_type=MESH)
    pl.semaphore_signal(barrier, inc=1, device_id={"ctx": sibling}, device_id_type=MESH)
    for d in range(1, n_page):
        pl.semaphore_signal(
            barrier, inc=1, device_id={"page": (page + d) % n_page}, device_id_type=MESH
        )

    local = []

    def fetch(src, dst, j):
        copy = pltpu.make_async_copy(src, dst, own_sem.at[j])
        copy.start()
        local.append(copy)

    fetch(q_in, q_ref, 0)
    fetch(k_in, own.at[0], 1)
    fetch(v_in, own.at[1], 2)
    fetch(table_in, table_ref, 3)
    fetch(slots_in, slots_ref, 4)

    rows_at = lax.broadcasted_iota(jnp.int32, (SPAN, wide), 1) % SPAN
    keys_at = lax.broadcasted_iota(jnp.int32, (SPAN, wide), 0)
    vt[DH:, :] = jnp.ones((vt.shape[0] - DH, vt.shape[1]), jnp.bfloat16)
    for copy in local:
        copy.wait()
    mine = []
    for p in range(count):
        copy = pltpu.make_async_copy(
            own.at[:, :, pl.ds(starts[p], PIECES[p])], bufs[p].at[me], own_sem.at[5 + p]
        )
        copy.start()
        mine.append(copy)

    for i in range(spans):
        here = table_ref[me * spans + i]
        for t in range(spans):
            own_bias[i * spans + t] = jnp.where(table_ref[me * spans + t] < here, 0.0, HIDE)
        for d in range(1, n):
            for t in range(spans):
                there = table_ref[((me + d) % n) * spans + t]
                bias[(i * (n - 1) + d - 1) * spans + t] = jnp.where(there < here, 0.0, HIDE)

    @pl.loop(0, pairs)
    def _(g):
        for i in range(spans):
            for h in range(PAIR):
                place = pl.ds(pl.multiple_of((g * PAIR + h) * DH, DH), DH)
                value = q_ref[pl.ds(i * SPAN, SPAN), place].astype(jnp.float32) * rate
                high = value.astype(jnp.bfloat16)
                qs[g * spans + i, h * SPAN : (h + 1) * SPAN, :DH] = high
                qs[g * spans + i, h * SPAN : (h + 1) * SPAN, DH:] = (
                    value - high.astype(jnp.float32)
                ).astype(jnp.bfloat16)

    def attention(size, rows, first):
        blocks = size // rows
        steps = rows // 8

        def shift(i, t):
            return own_bias[i * spans + t] if first else bias[i * blocks + t]

        def score(u, i, s):
            keys = kc[:size]
            value = lax.dot_general(
                jnp.concatenate([keys, keys], axis=1), qs[u],
                (((1,), (1,)), ((), ())), preferred_element_type=jnp.float32,
            )
            best = None
            for t in range(blocks):
                part = value[t * rows : (t + 1) * rows]
                if first and t == i:
                    part = jnp.where(keys_at > rows_at, HIDE, part)
                s[t * rows : (t + 1) * rows] = part
                high = part[:8]
                for r in range(1, steps):
                    high = jnp.maximum(high, part[r * 8 : (r + 1) * 8])
                if not (first and t == i):
                    high = high + shift(i, t)
                best = high if best is None else jnp.maximum(best, high)
            best = jnp.broadcast_to(jnp.max(best, axis=0, keepdims=True), (8, wide))
            if first:
                tops[u] = best
                return best, best
            old = tops[u]
            new = jnp.maximum(old, best)
            tops[u] = new
            return new, jnp.exp2(old - new)

        def weigh(i, high, s, w):
            for t in range(blocks):
                level = high if first and t == i else high - shift(i, t)
                level = jnp.concatenate([level] * steps, axis=0)
                w[t * rows : (t + 1) * rows] = jnp.exp2(
                    s[t * rows : (t + 1) * rows] - level
                ).astype(jnp.bfloat16)

        def gather(u, factor, w):
            update = jnp.dot(vt[:, :size], w[:size], preferred_element_type=jnp.float32)
            update = update[: DH + 8]
            if first:
                acc[u] = update
            else:
                acc[u] = acc[u] * jnp.concatenate([factor] * (DH // 8 + 1), axis=0) + update

        per = math.gcd(pairs, max(1, 8 * 512 // (spans * size))) * spans
        ss, ww = (s0, s1), (p0, p1)

        def body(j, carry):
            (high, factor), late = carry
            for x in range(per):
                u = per * j + x
                now = x % 2
                weigh(x % spans, high, ss[now], ww[now])
                after = score((u + 1) % units, (x + 1) % spans, ss[1 - now])
                before = u - 1 if x else lax.rem(u + units, units + 1)
                gather(before, late, ww[1 - now])
                late = factor
                high, factor = after
            return (high, factor), late

        start = score(0, 0, s0)
        carry = lax.fori_loop(0, units // per, body, (start, start[1]))
        gather(units - 1, carry[1], ww[(per - 1) % 2])

    size = spans * SPAN
    kc[:size] = own[0].reshape(size, DH)
    vt[:DH, :size] = own[1].reshape(size, DH).T
    attention(size, SPAN, True)

    pl.semaphore_wait(barrier, chips + n_page - 1)

    def remote(p, src, owner, index, target):
        return pltpu.make_async_remote_copy(
            src_ref=src,
            dst_ref=bufs[p].at[owner],
            send_sem=send.at[p, index],
            recv_sem=recv.at[p, index],
            device_id={"ctx": target},
            device_id_type=MESH,
        )

    started = []
    for p in range(count):
        part = own.at[:, :, pl.ds(starts[p], PIECES[p])]
        for d in range(1, chips):
            copy = remote(p, part, me, d, ahead(d))
            copy.start()
            started.append(copy)
        copy = remote(p, part, me, 0, sibling)
        copy.start()
        started.append(copy)

    wanted = []
    for s in range(spans):
        device, place = jnp.int32(0), jnp.int32(0)
        for g in range(n * spans):
            hit = slots_ref[g] == me * spans + s
            device = jnp.where(hit, g // spans, device)
            place = jnp.where(hit, g % spans, place)
        wanted.append((device, place))

    def collect(p):
        buf = bufs[p]
        for d in range(1, chips):
            origin = behind(d, core)
            remote(p, buf.at[origin], origin, d, sibling).wait_recv()
            copy = remote(p, buf.at[origin], origin, chips - 1 + d, sibling)
            copy.start()
            started.append(copy)
        mine[p].wait()
        remote(p, buf.at[sibling], sibling, 0, sibling).wait_recv()
        for d in range(1, chips):
            origin = behind(d, 1 - core)
            remote(p, buf.at[origin], origin, chips - 1 + d, sibling).wait_recv()

    def page_copy(p, index, target, origin):
        ref = zbufs[p].at[origin]
        return pltpu.make_async_remote_copy(
            src_ref=ref,
            dst_ref=ref,
            send_sem=page_send.at[p, index],
            recv_sem=page_recv.at[p, index],
            device_id={"page": target},
            device_id_type=MESH,
        )

    def select(p):
        for s in range(spans):
            device, place = wanted[s]
            for j in range(2):
                zbufs[p][page, j, s] = bufs[p][device, j, place]

    def publish(p):
        for index in range(1, n_page):
            copy = page_copy(p, index, (page + index) % n_page, page)
            copy.start()
            started.append(copy)

    for p in range(count):
        rows = PIECES[p]
        size = (n - 1) * spans * rows
        collect(p)
        select(p)
        other = []
        for d in range(1, n):
            for t in range(spans):
                place = ((d - 1) * spans + t) * rows
                kc[place : place + rows] = bufs[p][(me + d) % n, 0, t]
                other.append(bufs[p][(me + d) % n, 1, t])
        publish(p)
        vt[:DH, :size] = jnp.concatenate(other, axis=0).T
        attention(size, rows, False)

    @pl.loop(0, pairs)
    def _(g):
        for i in range(spans):
            u = g * spans + i
            total = jnp.concatenate([acc[u, DH : DH + 8]] * (DH // 8), axis=0)
            value = (acc[u, :DH] / total).T
            for h in range(PAIR):
                place = pl.ds(pl.multiple_of((g * PAIR + h) * DH, DH), DH)
                att[pl.ds(i * SPAN, SPAN), place] = value[h * SPAN : (h + 1) * SPAN].astype(
                    jnp.bfloat16
                )

    finish = pltpu.make_async_copy(att, att_out, out_sem.at[0])
    finish.start()

    for p in range(count):
        for index in range(1, n_page):
            origin = (page + n_page - index) % n_page
            page_copy(p, index, page, origin).wait_recv()

    lanes = lax.broadcasted_iota(jnp.int32, (8, DH), 1)
    for s in range(spans):
        for j in range(2):
            levels = jnp.zeros((8, DH), jnp.float32)
            for h in range(n_page):
                level = None
                for p in range(count):
                    high = jnp.max(jnp.abs(zbufs[p][h, j, s].astype(jnp.float32)), axis=0, keepdims=True)
                    level = high if level is None else jnp.maximum(level, high)
                level = jnp.max(level, axis=1, keepdims=True) + 1e-06
                for p in range(count):
                    cache[s, h, j, starts[p] : starts[p] + PIECES[p]] = (
                        zbufs[p][h, j, s].astype(jnp.float32) / level
                    ).astype(jnp.bfloat16)
                levels = jnp.where(lanes == h, level, levels)
            scales[s, j] = levels
    last = [
        pltpu.make_async_copy(cache, cache_out, out_sem.at[1]),
        pltpu.make_async_copy(scales, scales_out, out_sem.at[2]),
    ]
    for copy in last:
        copy.start()
    for copy in started:
        copy.wait_send()
    finish.wait()
    for copy in last:
        copy.wait()


def place_results(att_in, cache_in, scales_in, att_out, cache_out, scales_out, att, cache, sems):
    parts = 4
    rows = att.shape[0] // parts
    moves = []
    for j in range(parts):
        place = pl.ds(j * rows, rows)
        moves.append((att_in.at[place], att.at[place], att_out.at[place]))
    for s in range(cache.shape[0]):
        moves.append((cache_in.at[s], cache.at[s], cache_out.at[s]))
    ins = [pltpu.make_async_copy(a, b, sems.at[0, j]) for j, (a, b, _) in enumerate(moves)]
    outs = [pltpu.make_async_copy(b, c, sems.at[1, j]) for j, (_, b, c) in enumerate(moves)]
    for copy in ins:
        copy.start()
    for s in range(scales_out.shape[0]):
        for j in range(scales_out.shape[1]):
            scales_out[s, j : j + 1] = scales_in[s, j, :1, : scales_out.shape[2]]
    for a, b in zip(ins, outs):
        a.wait()
        b.start()
    for copy in outs:
        copy.wait()


def on_device(n, n_page, queries, keys, values, span_table, page_slots):
    rows = queries.shape[0]
    heads = queries.shape[1] // DH
    spans = rows // SPAN
    units = heads // PAIR * spans
    wide = PAIR * SPAN
    most = max(spans * SPAN, max((n - 1) * spans * p for p in PIECES))
    padded = -(-most // 128) * 128
    any_space = pl.BlockSpec(memory_space=pl.ANY)
    vmem = pl.BlockSpec(memory_space=pltpu.VMEM)
    count = len(PIECES)
    results = (
        jax.ShapeDtypeStruct((rows, heads * DH), jnp.bfloat16),
        jax.ShapeDtypeStruct((spans, n_page, 2, PAGE, DH), jnp.bfloat16),
        jax.ShapeDtypeStruct((spans, 2, 8, DH), jnp.float32),
    )
    attended, cache, scales = pl.pallas_call(
        functools.partial(kernel, n, n_page, heads, spans),
        out_shape=results,
        in_specs=[any_space] * 5,
        out_specs=(any_space,) * 3,
        scratch_shapes=[
            pltpu.SMEM(span_table.shape, jnp.int32),
            pltpu.SMEM(page_slots.shape, jnp.int32),
            pltpu.SMEM((spans * (n - 1) * spans,), jnp.float32),
            pltpu.SMEM((spans * spans,), jnp.float32),
            pltpu.VMEM(queries.shape, jnp.bfloat16),
            pltpu.VMEM((2, spans, SPAN, DH), jnp.bfloat16),
            pltpu.VMEM((units, wide, 2 * DH), jnp.bfloat16),
            pltpu.VMEM((most, DH), jnp.bfloat16),
            pltpu.VMEM((DH + 16, padded), jnp.bfloat16),
            pltpu.VMEM((most, wide), jnp.float32),
            pltpu.VMEM((most, wide), jnp.float32),
            pltpu.VMEM((most, wide), jnp.bfloat16),
            pltpu.VMEM((most, wide), jnp.bfloat16),
            pltpu.VMEM((units, 8, wide), jnp.float32),
            pltpu.VMEM((units + 1, DH + 8, wide), jnp.float32),
            pltpu.VMEM(queries.shape, jnp.bfloat16),
            pltpu.VMEM((spans, n_page, 2, PAGE, DH), jnp.bfloat16),
            pltpu.VMEM((spans, 2, 8, DH), jnp.float32),
            pltpu.SemaphoreType.DMA((count, n)),
            pltpu.SemaphoreType.DMA((count, n)),
            pltpu.SemaphoreType.DMA((5 + count,)),
            pltpu.SemaphoreType.DMA((count, n_page)),
            pltpu.SemaphoreType.DMA((count, n_page)),
            pltpu.SemaphoreType.DMA((3,)),
        ]
        + [pltpu.VMEM((n, 2, spans, p, DH), jnp.bfloat16) for p in PIECES]
        + [pltpu.VMEM((n_page, 2, spans, p, DH), jnp.bfloat16) for p in PIECES],
        compiler_params=pltpu.CompilerParams(
            collective_id=0, has_side_effects=True, vmem_limit_bytes=48 * 2**20
        ),
    )(
        span_table,
        page_slots,
        queries,
        keys.reshape(spans, SPAN, DH),
        values.reshape(spans, SPAN, DH),
    )
    attended, cache, scales = pl.pallas_call(
        place_results,
        out_shape=results[:2] + (jax.ShapeDtypeStruct((spans, 2, n_page), jnp.float32),),
        in_specs=[any_space, any_space, vmem],
        out_specs=(any_space, any_space, vmem),
        scratch_shapes=[
            pltpu.VMEM((rows, heads * DH), jnp.bfloat16),
            pltpu.VMEM((spans, n_page, 2, PAGE, DH), jnp.bfloat16),
            pltpu.SemaphoreType.DMA((2, 4 + spans)),
        ],
        compiler_params=pltpu.CompilerParams(vmem_limit_bytes=16 * 2**20),
    )(attended, cache, scales)
    return attended, cache, scales.transpose(0, 2, 1)


def solution(mesh):
    placed = (P("ctx", "page"), P("ctx", "page"), P("ctx", "page"), P(), P())
    return jax.shard_map(
        functools.partial(on_device, mesh.shape["ctx"], mesh.shape["page"]),
        mesh=mesh,
        in_specs=placed,
        out_specs=(P("ctx", "page"), P("ctx", None, None, None, None), P("ctx", None, None)),
        check_vma=False,
    )
```

```python
import functools
import math

import jax
import jax.numpy as jnp
from jax import lax
from jax.experimental import pallas as pl
from jax.experimental.pallas import tpu as pltpu
from jax.sharding import PartitionSpec as P

DH = 128
PAGE = 128
SPAN = 128
HIDE = -1e30
PAIR = 2
PIECES = (32, 32, 32, 32)
MESH = pl.DeviceIdType.MESH


def kernel(
    n, n_page, heads, spans, table_in, slots_in, q_in, k_in, v_in,
    att_out, cache_out, scales_out,
    table_ref, slots_ref, bias, q_ref, own, vts, s0, s1, p0, p1,
    tops, acc, att, cache, scales, send, recv, own_sem, page_send, page_recv, out_sem,
    *pieces,
):
    count = len(PIECES)
    bufs, zbufs = pieces[:count], pieces[count:]
    starts = [sum(PIECES[:p]) for p in range(count)]
    chips = n // 2
    pairs = heads // PAIR
    wide = PAIR * SPAN
    units = pairs * spans
    me = lax.axis_index("ctx")
    page = lax.axis_index("page")
    chip = me // 2
    core = me % 2
    sibling = 2 * chip + 1 - core
    rate = DH ** (-0.5) * math.log2(math.e)

    def ahead(d):
        return 2 * ((chip + d) % chips) + core

    def behind(d, c):
        return 2 * ((chip + chips - d) % chips) + c

    barrier = pltpu.get_barrier_semaphore()
    for d in range(1, chips):
        pl.semaphore_signal(barrier, inc=1, device_id={"ctx": ahead(d)}, device_id_type=MESH)
    pl.semaphore_signal(barrier, inc=1, device_id={"ctx": sibling}, device_id_type=MESH)
    for d in range(1, n_page):
        pl.semaphore_signal(
            barrier, inc=1, device_id={"page": (page + d) % n_page}, device_id_type=MESH
        )

    local = []

    def fetch(src, dst, j):
        copy = pltpu.make_async_copy(src, dst, own_sem.at[j])
        copy.start()
        local.append(copy)

    fetch(q_in, q_ref, 0)
    fetch(k_in, own.at[0], 1)
    fetch(v_in, own.at[1], 2)
    fetch(table_in, table_ref, 3)
    fetch(slots_in, slots_ref, 4)

    rows_at = lax.broadcasted_iota(jnp.int32, (SPAN, wide), 1) % SPAN
    keys_at = lax.broadcasted_iota(jnp.int32, (SPAN, wide), 0)
    for vt in vts:
        vt[DH:, :] = jnp.ones((vt.shape[0] - DH, vt.shape[1]), jnp.bfloat16)
    for copy in local:
        copy.wait()
    mine = []
    for p in range(count):
        copy = pltpu.make_async_copy(
            own.at[:, :, pl.ds(starts[p], PIECES[p])], bufs[p].at[me], own_sem.at[5 + p]
        )
        copy.start()
        mine.append(copy)

    order = [me, sibling]
    for d in range(1, chips):
        order += [behind(d, core), behind(d, 1 - core)]
    for i in range(spans):
        here = table_ref[me * spans + i]
        for d, device in enumerate(order):
            for t in range(spans):
                there = table_ref[device * spans + t]
                bias[(i * n + d) * spans + t] = jnp.where(there < here, 0.0, HIDE)

    class Chunk:
        def __init__(self, parts, rows, base, vt, diagonal):
            self.parts = parts
            self.rows = rows
            self.base = base
            self.vt = vt
            self.diagonal = diagonal
            self.blocks = len(parts) * spans
            self.size = self.blocks * rows

        def stage(self):
            other = [part(1, t) for part in self.parts for t in range(spans)]
            self.vt[:DH, : self.size] = jnp.concatenate(other, axis=0).T

        def keys(self):
            return jnp.concatenate(
                [part(0, t) for part in self.parts for t in range(spans)], axis=0
            )

        def shift(self, i, t):
            if self.diagonal and t == i:
                return None
            return bias[i * n * spans + self.base * spans + t]

    def pair_of(u, i):
        return (u - i) // spans if isinstance(u, int) else lax.div(u - i, spans)

    def score(chunk, u, i, s):
        g = pair_of(u, i)
        query = jnp.concatenate(
            [
                q_ref[
                    pl.ds(i * SPAN, SPAN),
                    pl.ds(pl.multiple_of((g * PAIR + h) * DH, DH), DH),
                ]
                for h in range(PAIR)
            ],
            axis=0,
        )
        value = lax.dot_general(
            chunk.keys(), query, (((1,), (1,)), ((), ())), preferred_element_type=jnp.float32
        )
        best = None
        rows = chunk.rows
        for t in range(chunk.blocks):
            part = value[t * rows : (t + 1) * rows]
            offset = chunk.shift(i, t)
            if offset is None:
                part = jnp.where(keys_at > rows_at, HIDE, part)
            s[t * rows : (t + 1) * rows] = part
            high = part[:8]
            for r in range(1, rows // 8):
                high = jnp.maximum(high, part[r * 8 : (r + 1) * 8])
            if offset is not None:
                high = high + offset
            best = high if best is None else jnp.maximum(best, high)
        best = jnp.broadcast_to(jnp.max(best, axis=0, keepdims=True), (8, wide))
        if chunk.diagonal:
            tops[u] = best
            return best, best
        old = tops[u]
        new = jnp.maximum(old, best)
        tops[u] = new
        return new, jnp.exp2((old - new) * rate)

    def weigh(chunk, i, high, s, w):
        rows = chunk.rows
        for t in range(chunk.blocks):
            offset = chunk.shift(i, t)
            level = high if offset is None else high - offset
            level = jnp.concatenate([level] * (rows // 8), axis=0)
            w[t * rows : (t + 1) * rows] = jnp.exp2(
                (s[t * rows : (t + 1) * rows] - level) * rate
            ).astype(jnp.bfloat16)

    def gather(chunk, u, factor, w):
        update = jnp.dot(
            chunk.vt[:, : chunk.size], w[: chunk.size], preferred_element_type=jnp.float32
        )
        update = update[: DH + 8]
        if not chunk.diagonal:
            update = acc[u] * jnp.concatenate([factor] * (DH // 8 + 1), axis=0) + update
        acc[u] = update
        return update

    def finish_unit(u, i, value):
        g = pair_of(u, i)
        share = 1.0 / value[DH : DH + 8]
        value = (value[:DH] * jnp.concatenate([share] * (DH // 8), axis=0)).T
        for h in range(PAIR):
            att[
                pl.ds(i * SPAN, SPAN), pl.ds(pl.multiple_of((g * PAIR + h) * DH, DH), DH)
            ] = value[h * SPAN : (h + 1) * SPAN].astype(jnp.bfloat16)

    ss, ww = (s0, s1), (p0, p1)

    def steps_of(chunk):
        most = max(1, 8 * 512 // (spans * chunk.size))
        return max(k for k in range(1, most + 1) if pairs % k == 0) * spans

    def attend(group, between, final):
        per = steps_of(group[0])
        turns = units // per

        def turn(j, carry, c, head, tail):
            chunk = group[c]
            (high, factor), late = carry
            for x in range(per):
                u = per * j + x
                now = x % 2
                weigh(chunk, x % spans, high, ss[now], ww[now])
                if x < per - 1 or not tail:
                    after = score(chunk, u + 1, (x + 1) % spans, ss[1 - now])
                elif c + 1 < len(group):
                    after = score(group[c + 1], 0, 0, ss[1 - now])
                else:
                    after = (high, factor)
                if x or not head:
                    value = gather(chunk, u - 1, late, ww[1 - now])
                    if x and final and c == len(group) - 1:
                        finish_unit(u - 1, (x - 1) % spans, value)
                elif c:
                    gather(group[c - 1], units - 1, late, ww[1 - now])
                late = factor
                high, factor = after
            return (high, factor), late

        group[0].stage()
        start = score(group[0], 0, 0, s0)
        carry = start, start[1]
        for c in range(len(group)):
            if turns > 1:
                carry = turn(0, carry, c, True, False)
                if turns > 2:
                    carry = lax.fori_loop(
                        1,
                        turns - 1,
                        lambda j, carry, c=c: turn(j, carry, c, False, False),
                        carry,
                    )
            if c + 1 < len(group):
                between(c + 1)
                group[c + 1].stage()
            carry = turn(turns - 1, carry, c, turns == 1, True)
        value = gather(group[-1], units - 1, carry[1], ww[(per - 1) % 2])
        if final:
            finish_unit(units - 1, spans - 1, value)

            for j in range(turns - 1):
                u = per * j + per - 1
                finish_unit(u, spans - 1, acc[u])

    attend([Chunk([lambda j, t: own[j, t]], SPAN, 0, vts[0], True)], None, False)

    pl.semaphore_wait(barrier, chips + n_page - 1)

    def remote(p, src, owner, index, target):
        return pltpu.make_async_remote_copy(
            src_ref=src,
            dst_ref=bufs[p].at[owner],
            send_sem=send.at[p, index],
            recv_sem=recv.at[p, index],
            device_id={"ctx": target},
            device_id_type=MESH,
        )

    started = []
    for p in range(count):
        part = own.at[:, :, pl.ds(starts[p], PIECES[p])]
        for d in range(1, chips):
            copy = remote(p, part, me, d, ahead(d))
            copy.start()
            started.append(copy)
        copy = remote(p, part, me, 0, sibling)
        copy.start()
        started.append(copy)

    wanted = []
    for s in range(spans):
        device, place = jnp.int32(0), jnp.int32(0)
        for g in range(n * spans):
            hit = slots_ref[g] == me * spans + s
            device = jnp.where(hit, g // spans, device)
            place = jnp.where(hit, g % spans, place)
        wanted.append((device, place))

    def collect(p):
        buf = bufs[p]
        for d in range(1, chips):
            origin = behind(d, core)
            remote(p, buf.at[origin], origin, d, sibling).wait_recv()
            copy = remote(p, buf.at[origin], origin, chips - 1 + d, sibling)
            copy.start()
            started.append(copy)
        for d in range(1, chips):
            origin = behind(d, 1 - core)
            remote(p, buf.at[origin], origin, chips - 1 + d, sibling).wait_recv()
        select(p)
        publish(p)

    def page_copy(p, index, target, origin):
        ref = zbufs[p].at[origin]
        return pltpu.make_async_remote_copy(
            src_ref=ref,
            dst_ref=ref,
            send_sem=page_send.at[p, index],
            recv_sem=page_recv.at[p, index],
            device_id={"page": target},
            device_id_type=MESH,
        )

    def select(p):
        for s in range(spans):
            device, place = wanted[s]
            for j in range(2):
                zbufs[p][page, j, s] = bufs[p][device, j, place]

    def publish(p):
        for index in range(1, n_page):
            copy = page_copy(p, index, (page + index) % n_page, page)
            copy.start()
            started.append(copy)

    for p in range(count):
        mine[p].wait()
        remote(p, bufs[p].at[sibling], sibling, 0, sibling).wait_recv()

    def beside(j, t):
        return jnp.concatenate([bufs[p][sibling, j, t] for p in range(count)], axis=0)

    attend([Chunk([beside], SPAN, 1, vts[0], False)], None, False)

    collect(0)
    group = [
        Chunk(
            [lambda j, t, p=p, device=device: bufs[p][device, j, t] for device in order[2:]],
            PIECES[p], 2, vts[p % 2], False,
        )
        for p in range(count)
    ]
    attend(group, collect, True)

    finish = pltpu.make_async_copy(att, att_out, out_sem.at[0])
    finish.start()

    for p in range(count):
        for index in range(1, n_page):
            origin = (page + n_page - index) % n_page
            page_copy(p, index, page, origin).wait_recv()

    lanes = lax.broadcasted_iota(jnp.int32, (8, DH), 1)
    for s in range(spans):
        for j in range(2):
            levels = jnp.zeros((8, DH), jnp.float32)
            for h in range(n_page):
                level = None
                for p in range(count):
                    high = jnp.max(jnp.abs(zbufs[p][h, j, s].astype(jnp.float32)), axis=0, keepdims=True)
                    level = high if level is None else jnp.maximum(level, high)
                level = jnp.max(level, axis=1, keepdims=True) + 1e-06
                share = 1.0 / level
                for p in range(count):
                    cache[s, h, j, starts[p] : starts[p] + PIECES[p]] = (
                        zbufs[p][h, j, s].astype(jnp.float32) * share
                    ).astype(jnp.bfloat16)
                levels = jnp.where(lanes == h, level, levels)
            scales[s, j] = levels
    last = [
        pltpu.make_async_copy(cache, cache_out, out_sem.at[1]),
        pltpu.make_async_copy(scales, scales_out, out_sem.at[2]),
    ]
    for copy in last:
        copy.start()
    for copy in started:
        copy.wait_send()
    finish.wait()
    for copy in last:
        copy.wait()


def place_results(att_in, cache_in, scales_in, att_out, cache_out, scales_out, sems):
    moves = [
        pltpu.make_async_copy(att_in, att_out, sems.at[0]),
        pltpu.make_async_copy(cache_in, cache_out, sems.at[1]),
    ]
    for copy in moves:
        copy.start()
    for s in range(scales_out.shape[0]):
        for j in range(scales_out.shape[1]):
            scales_out[s, j : j + 1] = scales_in[s, j, :1, : scales_out.shape[2]]
    for copy in moves:
        copy.wait()


def on_device(n, n_page, queries, keys, values, span_table, page_slots):
    rows = queries.shape[0]
    heads = queries.shape[1] // DH
    spans = rows // SPAN
    units = heads // PAIR * spans
    wide = PAIR * SPAN
    most = max(spans * SPAN, max((n - 2) * spans * p for p in PIECES))
    padded = -(-most // 128) * 128
    any_space = pl.BlockSpec(memory_space=pl.ANY)
    vmem = pl.BlockSpec(memory_space=pltpu.VMEM)
    hbm = pl.BlockSpec(memory_space=pltpu.HBM)
    count = len(PIECES)
    results = (
        jax.ShapeDtypeStruct((rows, heads * DH), jnp.bfloat16),
        jax.ShapeDtypeStruct((spans, n_page, 2, PAGE, DH), jnp.bfloat16),
        jax.ShapeDtypeStruct((spans, 2, 8, DH), jnp.float32),
    )
    attended, cache, scales = pl.pallas_call(
        functools.partial(kernel, n, n_page, heads, spans),
        out_shape=results,
        in_specs=[hbm] * 5,
        out_specs=(any_space,) * 3,
        scratch_shapes=[
            pltpu.SMEM(span_table.shape, jnp.int32),
            pltpu.SMEM(page_slots.shape, jnp.int32),
            pltpu.SMEM((spans * n * spans,), jnp.float32),
            pltpu.VMEM(queries.shape, jnp.bfloat16),
            pltpu.VMEM((2, spans, SPAN, DH), jnp.bfloat16),
            [pltpu.VMEM((DH + 16, padded), jnp.bfloat16)] * 2,
            pltpu.VMEM((most, wide), jnp.float32),
            pltpu.VMEM((most, wide), jnp.float32),
            pltpu.VMEM((most, wide), jnp.bfloat16),
            pltpu.VMEM((most, wide), jnp.bfloat16),
            pltpu.VMEM((units, 8, wide), jnp.float32),
            pltpu.VMEM((units, DH + 8, wide), jnp.float32),
            pltpu.VMEM(queries.shape, jnp.bfloat16),
            pltpu.VMEM((spans, n_page, 2, PAGE, DH), jnp.bfloat16),
            pltpu.VMEM((spans, 2, 8, DH), jnp.float32),
            pltpu.SemaphoreType.DMA((count, n)),
            pltpu.SemaphoreType.DMA((count, n)),
            pltpu.SemaphoreType.DMA((5 + count,)),
            pltpu.SemaphoreType.DMA((count, n_page)),
            pltpu.SemaphoreType.DMA((count, n_page)),
            pltpu.SemaphoreType.DMA((3,)),
        ]
        + [pltpu.VMEM((n, 2, spans, p, DH), jnp.bfloat16) for p in PIECES]
        + [pltpu.VMEM((n_page, 2, spans, p, DH), jnp.bfloat16) for p in PIECES],
        compiler_params=pltpu.CompilerParams(
            collective_id=0, has_side_effects=True, vmem_limit_bytes=48 * 2**20
        ),
    )(
        *(
            pltpu.with_memory_space_constraint(x, pltpu.HBM)
            for x in (
                span_table,
                page_slots,
                queries,
                keys.reshape(spans, SPAN, DH),
                values.reshape(spans, SPAN, DH),
            )
        )
    )
    attended, cache, scales = pl.pallas_call(
        place_results,
        out_shape=results[:2] + (jax.ShapeDtypeStruct((spans, 2, n_page), jnp.float32),),
        in_specs=[any_space, any_space, vmem],
        out_specs=(any_space, any_space, vmem),
        scratch_shapes=[
            pltpu.SemaphoreType.DMA((2,)),
        ],
        compiler_params=pltpu.CompilerParams(vmem_limit_bytes=16 * 2**20),
    )(attended, cache, scales)
    return attended, cache, scales.transpose(0, 2, 1)


def solution(mesh):
    placed = (P("ctx", "page"), P("ctx", "page"), P("ctx", "page"), P(), P())
    return jax.shard_map(
        functools.partial(on_device, mesh.shape["ctx"], mesh.shape["page"]),
        mesh=mesh,
        in_specs=placed,
        out_specs=(P("ctx", "page"), P("ctx", None, None, None, None), P("ctx", None, None)),
        check_vma=False,
    )
```

```python
import functools
import math

import jax
import jax.numpy as jnp
from jax import lax
from jax.experimental import pallas as pl
from jax.experimental.pallas import tpu as pltpu
from jax.sharding import PartitionSpec as P

DH = 128
PAGE = 128
SPAN = 128
HIDE = -1e30
PAIR = 2
PIECES = (32, 32, 32, 32)
MESH = pl.DeviceIdType.MESH


def kernel(
    n, n_page, heads, spans, table_in, slots_in, q_in, k_in, v_in,
    att_out, cache_out, scales_out,
    table_ref, slots_ref, bias, q_ref, own, vts, s0, s1, p0, p1,
    tops, acc, att, cache, scales, send, recv, own_sem, page_send, page_recv, far_send, far_recv, out_sem, fbuf,
    *pieces,
):
    count = len(PIECES)
    bufs, zbufs = pieces[:count], pieces[count:]
    starts = [sum(PIECES[:p]) for p in range(count)]
    chips = n // 2
    pairs = heads // PAIR
    wide = PAIR * SPAN
    units = pairs * spans
    me = lax.axis_index("ctx")
    page = lax.axis_index("page")
    chip = me // 2
    core = me % 2
    sibling = 2 * chip + 1 - core
    rate = DH ** (-0.5) * math.log2(math.e)

    def ahead(d):
        return 2 * ((chip + d) % chips) + core

    def behind(d, c):
        return 2 * ((chip + chips - d) % chips) + c

    barrier = pltpu.get_barrier_semaphore()
    for d in range(1, chips):
        pl.semaphore_signal(barrier, inc=1, device_id={"ctx": ahead(d)}, device_id_type=MESH)
    pl.semaphore_signal(barrier, inc=1, device_id={"ctx": sibling}, device_id_type=MESH)
    for d in range(1, n_page):
        pl.semaphore_signal(
            barrier, inc=1, device_id={"page": (page + d) % n_page}, device_id_type=MESH
        )

    local = []

    def fetch(src, dst, j):
        copy = pltpu.make_async_copy(src, dst, own_sem.at[j])
        copy.start()
        local.append(copy)

    fetch(k_in, own.at[0], 0)
    fetch(v_in, own.at[1], 1)
    fetch(table_in, table_ref, 2)
    fetch(q_in, q_ref, 3)
    fetch(slots_in, slots_ref, 4)

    pl.semaphore_wait(barrier, chips + n_page - 1)

    def remote(p, src, owner, index, target):
        return pltpu.make_async_remote_copy(
            src_ref=src,
            dst_ref=bufs[p].at[owner],
            send_sem=send.at[p, index],
            recv_sem=recv.at[p, index],
            device_id={"ctx": target},
            device_id_type=MESH,
        )

    started = []

    def launch(copy):
        copy.start()
        started.append(copy)

    def await_piece(p, owner, index):
        remote(p, bufs[p].at[owner], owner, index, sibling).wait_recv()

    def piece_of(p):
        return own.at[:, :, pl.ds(starts[p], PIECES[p])]

    def spread(p):
        for d in range(1, chips):
            launch(remote(p, piece_of(p), me, d, ahead(d)))

    def across(index):
        return pltpu.make_async_remote_copy(
            src_ref=piece_of(count - 1),
            dst_ref=fbuf.at[me, n_page - index - 1],
            send_sem=page_send.at[count - 1, index],
            recv_sem=page_recv.at[count - 1, index],
            device_id={"page": (page + index) % n_page},
            device_id_type=MESH,
        )

    for copy in local[:2]:
        copy.wait()
    spread(0)
    for index in range(1, n_page):
        launch(across(index))
    for p in range(count):
        launch(remote(p, piece_of(p), me, 0, sibling))

    rows_at = lax.broadcasted_iota(jnp.int32, (SPAN, wide), 1) % SPAN
    keys_at = lax.broadcasted_iota(jnp.int32, (SPAN, wide), 0)
    for vt in vts:
        vt[DH:, :] = jnp.ones((vt.shape[0] - DH, vt.shape[1]), jnp.bfloat16)
    for copy in local[2:]:
        copy.wait()
    mine = []
    for p in range(count):
        copy = pltpu.make_async_copy(piece_of(p), bufs[p].at[me], own_sem.at[5 + p])
        copy.start()
        mine.append(copy)

    order = [me, sibling]
    for d in range(1, chips):
        order += [behind(d, core), behind(d, 1 - core)]
    for i in range(spans):
        here = table_ref[me * spans + i]
        for d, device in enumerate(order):
            for t in range(spans):
                there = table_ref[device * spans + t]
                bias[(i * n + d) * spans + t] = jnp.where(there < here, 0.0, HIDE)

    class Chunk:
        def __init__(self, parts, rows, base, vt, diagonal):
            self.parts = parts
            self.rows = rows
            self.base = base
            self.vt = vt
            self.diagonal = diagonal
            self.blocks = len(parts) * spans
            self.size = self.blocks * rows

        def stage(self):
            other = [part(1, t) for part in self.parts for t in range(spans)]
            self.vt[:DH, : self.size] = jnp.concatenate(other, axis=0).T

        def keys(self):
            return jnp.concatenate(
                [part(0, t) for part in self.parts for t in range(spans)], axis=0
            )

        def shift(self, i, t):
            if self.diagonal and t == i:
                return None
            return bias[i * n * spans + self.base * spans + t]

    def pair_of(u, i):
        return (u - i) // spans if isinstance(u, int) else lax.div(u - i, spans)

    def score(chunk, u, i, s):
        g = pair_of(u, i)
        query = jnp.concatenate(
            [
                q_ref[
                    pl.ds(i * SPAN, SPAN),
                    pl.ds(pl.multiple_of((g * PAIR + h) * DH, DH), DH),
                ]
                for h in range(PAIR)
            ],
            axis=0,
        )
        value = lax.dot_general(
            chunk.keys(), query, (((1,), (1,)), ((), ())), preferred_element_type=jnp.float32
        )
        best = None
        rows = chunk.rows
        for t in range(chunk.blocks):
            part = value[t * rows : (t + 1) * rows]
            offset = chunk.shift(i, t)
            if offset is None:
                part = jnp.where(keys_at > rows_at, HIDE, part)
            s[t * rows : (t + 1) * rows] = part
            high = part[:8]
            for r in range(1, rows // 8):
                high = jnp.maximum(high, part[r * 8 : (r + 1) * 8])
            if offset is not None:
                high = high + offset
            best = high if best is None else jnp.maximum(best, high)
        best = jnp.broadcast_to(jnp.max(best, axis=0, keepdims=True), (8, wide))
        if chunk.diagonal:
            tops[u] = best
            return best, best
        old = tops[u]
        new = jnp.maximum(old, best)
        tops[u] = new
        return new, jnp.exp2((old - new) * rate)

    def weigh(chunk, i, high, s, w):
        rows = chunk.rows
        for t in range(chunk.blocks):
            offset = chunk.shift(i, t)
            level = high if offset is None else high - offset
            level = jnp.concatenate([level] * (rows // 8), axis=0)
            w[t * rows : (t + 1) * rows] = jnp.exp2(
                (s[t * rows : (t + 1) * rows] - level) * rate
            ).astype(jnp.bfloat16)

    def gather(chunk, u, factor, w):
        update = jnp.dot(
            chunk.vt[:, : chunk.size], w[: chunk.size], preferred_element_type=jnp.float32
        )
        update = update[: DH + 8]
        if not chunk.diagonal:
            update = acc[u] * jnp.concatenate([factor] * (DH // 8 + 1), axis=0) + update
        acc[u] = update
        return update

    def finish_unit(u, i, value):
        g = pair_of(u, i)
        share = 1.0 / value[DH : DH + 8]
        value = (value[:DH] * jnp.concatenate([share] * (DH // 8), axis=0)).T
        for h in range(PAIR):
            att[
                pl.ds(i * SPAN, SPAN), pl.ds(pl.multiple_of((g * PAIR + h) * DH, DH), DH)
            ] = value[h * SPAN : (h + 1) * SPAN].astype(jnp.bfloat16)

    ss, ww = (s0, s1), (p0, p1)

    def steps_of(chunk):
        most = min(pairs // 2, max(1, 8 * 512 // (spans * chunk.size)))
        return max(k for k in range(1, most + 1) if pairs % k == 0) * spans

    def attend(group, early, between, final):
        per = steps_of(group[0])
        turns = units // per

        def turn(j, carry, c, head, tail):
            chunk = group[c]
            (high, factor), late = carry
            for x in range(per):
                u = per * j + x
                now = x % 2
                weigh(chunk, x % spans, high, ss[now], ww[now])
                if x < per - 1 or not tail:
                    after = score(chunk, u + 1, (x + 1) % spans, ss[1 - now])
                elif c + 1 < len(group):
                    after = score(group[c + 1], 0, 0, ss[1 - now])
                else:
                    after = (high, factor)
                if x or not head:
                    value = gather(chunk, u - 1, late, ww[1 - now])
                    if x and final and c == len(group) - 1:
                        finish_unit(u - 1, (x - 1) % spans, value)
                elif c:
                    gather(group[c - 1], units - 1, late, ww[1 - now])
                late = factor
                high, factor = after
            return (high, factor), late

        group[0].stage()
        start = score(group[0], 0, 0, s0)
        carry = start, start[1]
        for c in range(len(group)):
            early(c)
            if turns > 1:
                carry = turn(0, carry, c, True, False)
                if turns > 2:
                    carry = lax.fori_loop(
                        1,
                        turns - 1,
                        lambda j, carry, c=c: turn(j, carry, c, False, False),
                        carry,
                    )
            between(c)
            if c + 1 < len(group):
                group[c + 1].stage()
            carry = turn(turns - 1, carry, c, turns == 1, True)
        value = gather(group[-1], units - 1, carry[1], ww[(per - 1) % 2])
        if final:
            finish_unit(units - 1, spans - 1, value)

            for j in range(turns - 1):
                u = per * j + per - 1
                finish_unit(u, spans - 1, acc[u])

    def idle(c):
        pass

    def spread_some(k):
        for p in range(1, count):
            if min(p, 3) == k:
                spread(p)

    attend(
        [Chunk([lambda j, t: own[j, t]], SPAN, 0, vts[0], True)],
        idle, lambda c: spread_some(1), False,
    )
    spread_some(2)

    wanted = []
    for s in range(spans):
        device, place = jnp.int32(0), jnp.int32(0)
        for g in range(n * spans):
            hit = slots_ref[g] == me * spans + s
            device = jnp.where(hit, g // spans, device)
            place = jnp.where(hit, g % spans, place)
        wanted.append((device, place))

    def relay(p):
        for d in range(1, chips):
            origin = behind(d, core)
            await_piece(p, origin, d)
            launch(remote(p, bufs[p].at[origin], origin, chips - 1 + d, sibling))

    def complete(p):
        for d in range(1, chips):
            await_piece(p, behind(d, 1 - core), chips - 1 + d)
        select(p)
        if p < count - 1:
            publish(p)

    def page_copy(p, index, target, origin):
        ref = zbufs[p].at[origin]
        return pltpu.make_async_remote_copy(
            src_ref=ref,
            dst_ref=ref,
            send_sem=page_send.at[p, index],
            recv_sem=page_recv.at[p, index],
            device_id={"page": target},
            device_id_type=MESH,
        )

    def select(p):
        for s in range(spans):
            device, place = wanted[s]
            for j in range(2):
                zbufs[p][page, j, s] = bufs[p][device, j, place]

    def publish(p):
        for index in range(1, n_page):
            launch(page_copy(p, index, (page + index) % n_page, page))

    def foreign(index, owner, target):
        ref = fbuf.at[owner]
        return pltpu.make_async_remote_copy(
            src_ref=ref,
            dst_ref=ref,
            send_sem=far_send.at[index],
            recv_sem=far_recv.at[index],
            device_id={"ctx": target},
            device_id_type=MESH,
        )

    def foreign_spread():
        for index in range(1, n_page):
            across(index).wait_recv()
        for d in range(1, chips):
            launch(foreign(d, me, ahead(d)))
        launch(foreign(0, me, sibling))

    def foreign_relay():
        for d in range(1, chips):
            origin = behind(d, core)
            foreign(d, origin, sibling).wait_recv()
            launch(foreign(chips - 1 + d, origin, sibling))

    def foreign_complete():
        foreign(0, sibling, sibling).wait_recv()
        for d in range(1, chips):
            foreign(chips - 1 + d, behind(d, 1 - core), sibling).wait_recv()
        for s in range(spans):
            device, place = wanted[s]
            for k in range(1, n_page):
                for j in range(2):
                    zbufs[count - 1][(page + k) % n_page, j, s] = fbuf[device, k - 1, j, place]

    for p in range(count):
        mine[p].wait()
        await_piece(p, sibling, 0)

    def beside(j, t):
        return jnp.concatenate([bufs[p][sibling, j, t] for p in range(count)], axis=0)

    def meet(c):
        spread_some(3)
        relay(0)

    attend([Chunk([beside], SPAN, 1, vts[0], False)], idle, meet, False)

    complete(0)
    group = [
        Chunk(
            [lambda j, t, p=p, device=device: bufs[p][device, j, t] for device in order[2:]],
            PIECES[p], 2, vts[p % 2], False,
        )
        for p in range(count)
    ]

    def early(c):
        if c == 0:
            relay(1)
        elif c == 1:
            complete(2)
            relay(3)
        elif c == 3:
            foreign_relay()

    def between(c):
        if c == 0:
            complete(1)
            foreign_spread()
            relay(2)
        elif c == 1:
            complete(3)

    attend(group, early, between, True)
    foreign_complete()

    finish = pltpu.make_async_copy(att, att_out, out_sem.at[0])
    finish.start()

    for p in range(count - 1):
        for index in range(1, n_page):
            page_copy(p, index, page, (page + n_page - index) % n_page).wait_recv()

    lanes = lax.broadcasted_iota(jnp.int32, (8, DH), 1)
    for s in range(spans):
        for j in range(2):
            levels = jnp.zeros((8, DH), jnp.float32)
            for h in range(n_page):
                level = None
                for p in range(count):
                    high = jnp.max(jnp.abs(zbufs[p][h, j, s].astype(jnp.float32)), axis=0, keepdims=True)
                    level = high if level is None else jnp.maximum(level, high)
                level = jnp.max(level, axis=1, keepdims=True) + 1e-06
                share = 1.0 / level
                for p in range(count):
                    cache[s, h, j, starts[p] : starts[p] + PIECES[p]] = (
                        zbufs[p][h, j, s].astype(jnp.float32) * share
                    ).astype(jnp.bfloat16)
                levels = jnp.where(lanes == h, level, levels)
            scales[s, j] = levels
    last = [
        pltpu.make_async_copy(cache, cache_out, out_sem.at[1]),
        pltpu.make_async_copy(scales, scales_out, out_sem.at[2]),
    ]
    for copy in last:
        copy.start()
    for copy in started:
        copy.wait_send()
    finish.wait()
    for copy in last:
        copy.wait()


def place_results(att_in, cache_in, scales_in, att_out, cache_out, scales_out, sems):
    parts = sems.shape[0] - cache_in.shape[0]
    rows = att_in.shape[0] // parts
    moves = [
        (att_in.at[pl.ds(j * rows, rows)], att_out.at[pl.ds(j * rows, rows)]) for j in range(parts)
    ]
    moves += [(cache_in.at[s], cache_out.at[s]) for s in range(cache_in.shape[0])]
    moves = [pltpu.make_async_copy(*pair, sems.at[j]) for j, pair in enumerate(moves)]
    for copy in moves:
        copy.start()
    for s in range(scales_out.shape[0]):
        for j in range(scales_out.shape[1]):
            scales_out[s, j : j + 1] = scales_in[s, j, :1, : scales_out.shape[2]]
    for copy in moves:
        copy.wait()


def on_device(n, n_page, queries, keys, values, span_table, page_slots):
    rows = queries.shape[0]
    heads = queries.shape[1] // DH
    spans = rows // SPAN
    units = heads // PAIR * spans
    wide = PAIR * SPAN
    most = max(spans * SPAN, max((n - 2) * spans * p for p in PIECES))
    padded = -(-most // 128) * 128
    any_space = pl.BlockSpec(memory_space=pl.ANY)
    vmem = pl.BlockSpec(memory_space=pltpu.VMEM)
    hbm = pl.BlockSpec(memory_space=pltpu.HBM)
    count = len(PIECES)
    results = (
        jax.ShapeDtypeStruct((rows, heads * DH), jnp.bfloat16),
        jax.ShapeDtypeStruct((spans, n_page, 2, PAGE, DH), jnp.bfloat16),
        jax.ShapeDtypeStruct((spans, 2, 8, DH), jnp.float32),
    )
    attended, cache, scales = pl.pallas_call(
        functools.partial(kernel, n, n_page, heads, spans),
        out_shape=results,
        in_specs=[hbm] * 5,
        out_specs=(any_space,) * 3,
        scratch_shapes=[
            pltpu.SMEM(span_table.shape, jnp.int32),
            pltpu.SMEM(page_slots.shape, jnp.int32),
            pltpu.SMEM((spans * n * spans,), jnp.float32),
            pltpu.VMEM(queries.shape, jnp.bfloat16),
            pltpu.VMEM((2, spans, SPAN, DH), jnp.bfloat16),
            [pltpu.VMEM((DH + 16, padded), jnp.bfloat16)] * 2,
            pltpu.VMEM((most, wide), jnp.float32),
            pltpu.VMEM((most, wide), jnp.float32),
            pltpu.VMEM((most, wide), jnp.bfloat16),
            pltpu.VMEM((most, wide), jnp.bfloat16),
            pltpu.VMEM((units, 8, wide), jnp.float32),
            pltpu.VMEM((units, DH + 8, wide), jnp.float32),
            pltpu.VMEM(queries.shape, jnp.bfloat16),
            pltpu.VMEM((spans, n_page, 2, PAGE, DH), jnp.bfloat16),
            pltpu.VMEM((spans, 2, 8, DH), jnp.float32),
            pltpu.SemaphoreType.DMA((count, n - 1)),
            pltpu.SemaphoreType.DMA((count, n - 1)),
            pltpu.SemaphoreType.DMA((5 + count,)),
            pltpu.SemaphoreType.DMA((count, n_page)),
            pltpu.SemaphoreType.DMA((count, n_page)),
            pltpu.SemaphoreType.DMA((n - 1,)),
            pltpu.SemaphoreType.DMA((n - 1,)),
            pltpu.SemaphoreType.DMA((3,)),
            pltpu.VMEM((n, n_page - 1, 2, spans, PIECES[-1], DH), jnp.bfloat16),
        ]
        + [pltpu.VMEM((n, 2, spans, p, DH), jnp.bfloat16) for p in PIECES]
        + [pltpu.VMEM((n_page, 2, spans, p, DH), jnp.bfloat16) for p in PIECES],
        compiler_params=pltpu.CompilerParams(
            collective_id=0, has_side_effects=True, vmem_limit_bytes=48 * 2**20
        ),
    )(
        *(
            pltpu.with_memory_space_constraint(x, pltpu.HBM)
            for x in (
                span_table,
                page_slots,
                queries,
                keys.reshape(spans, SPAN, DH),
                values.reshape(spans, SPAN, DH),
            )
        )
    )
    attended, cache, scales = pl.pallas_call(
        place_results,
        out_shape=results[:2] + (jax.ShapeDtypeStruct((spans, 2, n_page), jnp.float32),),
        in_specs=[any_space, any_space, vmem],
        out_specs=(any_space, any_space, vmem),
        scratch_shapes=[
            pltpu.SemaphoreType.DMA((4 + spans,)),
        ],
        compiler_params=pltpu.CompilerParams(vmem_limit_bytes=16 * 2**20),
    )(attended, cache, scales)
    return attended, cache, scales.transpose(0, 2, 1)


def solution(mesh):
    placed = (P("ctx", "page"), P("ctx", "page"), P("ctx", "page"), P(), P())
    return jax.shard_map(
        functools.partial(on_device, mesh.shape["ctx"], mesh.shape["page"]),
        mesh=mesh,
        in_specs=placed,
        out_specs=(P("ctx", "page"), P("ctx", None, None, None, None), P("ctx", None, None)),
        check_vma=False,
    )
```

```python
import functools
import math

import jax
import jax.numpy as jnp
from jax import lax
from jax.experimental import pallas as pl
from jax.experimental.pallas import tpu as pltpu
from jax.sharding import PartitionSpec as P

DH = 128
PAGE = 128
SPAN = 128
HIDE = -1e30
PAIR = 2
PIECES = (32, 32, 32, 32)
CHUNKS = ((0,), (1,), (2, 3))
MESH = pl.DeviceIdType.MESH


def kernel(
    n, n_page, heads, spans, table_in, slots_in, q_in, k_in, v_in,
    att_out, cache_out, scales_out,
    table_ref, slots_ref, bias, q_ref, own, vts, s0, s1, p0, p1,
    tops, acc, att, cache, scales, send, recv, own_sem, page_send, page_recv, far_send, far_recv, out_sem, fbuf,
    *pieces,
):
    count = len(PIECES)
    bufs, zbufs = pieces[:count], pieces[count:]
    starts = [sum(PIECES[:p]) for p in range(count)]
    chips = n // 2
    pairs = heads // PAIR
    wide = PAIR * SPAN
    units = pairs * spans
    me = lax.axis_index("ctx")
    page = lax.axis_index("page")
    chip = me // 2
    core = me % 2
    sibling = 2 * chip + 1 - core
    rate = DH ** (-0.5) * math.log2(math.e)

    def ahead(d):
        return 2 * ((chip + d) % chips) + core

    def behind(d, c):
        return 2 * ((chip + chips - d) % chips) + c

    barrier = pltpu.get_barrier_semaphore()
    for d in range(1, chips):
        pl.semaphore_signal(barrier, inc=1, device_id={"ctx": ahead(d)}, device_id_type=MESH)
    pl.semaphore_signal(barrier, inc=1, device_id={"ctx": sibling}, device_id_type=MESH)
    for d in range(1, n_page):
        pl.semaphore_signal(
            barrier, inc=1, device_id={"page": (page + d) % n_page}, device_id_type=MESH
        )

    local = []

    def fetch(src, dst, j):
        copy = pltpu.make_async_copy(src, dst, own_sem.at[j])
        copy.start()
        local.append(copy)

    fetch(k_in, own.at[0], 0)
    fetch(v_in, own.at[1], 1)
    fetch(table_in, table_ref, 2)
    fetch(q_in, q_ref, 3)
    fetch(slots_in, slots_ref, 4)

    pl.semaphore_wait(barrier, chips + n_page - 1)

    def remote(p, src, owner, index, target):
        return pltpu.make_async_remote_copy(
            src_ref=src,
            dst_ref=bufs[p].at[owner],
            send_sem=send.at[p],
            recv_sem=recv.at[p, index],
            device_id={"ctx": target},
            device_id_type=MESH,
        )

    def several(ref, copies, send_sem, recv_sem):
        some = ref.at[pl.ds(0, copies)]
        return pltpu.make_async_remote_copy(
            src_ref=some,
            dst_ref=some,
            send_sem=recv_sem if send_sem is None else send_sem,
            recv_sem=send_sem if recv_sem is None else recv_sem,
            device_id={"ctx": sibling},
            device_id_type=MESH,
        )

    def await_piece(p, owner, index):
        remote(p, bufs[p].at[owner], owner, index, sibling).wait_recv()

    def piece_of(p):
        return own.at[:, :, pl.ds(starts[p], PIECES[p])]

    def spread(p):
        for d in range(1, chips):
            remote(p, piece_of(p), me, d, ahead(d)).start()

    def across(index):
        return pltpu.make_async_remote_copy(
            src_ref=piece_of(count - 1),
            dst_ref=fbuf.at[me, n_page - index - 1],
            send_sem=page_send.at[count - 1],
            recv_sem=page_recv.at[count - 1],
            device_id={"page": (page + index) % n_page},
            device_id_type=MESH,
        )

    for copy in local[:2]:
        copy.wait()
    spread(0)
    for index in range(1, n_page):
        across(index).start()
    for p in range(count):
        remote(p, piece_of(p), me, 0, sibling).start()

    rows_at = lax.broadcasted_iota(jnp.int32, (SPAN, wide), 1) % SPAN
    keys_at = lax.broadcasted_iota(jnp.int32, (SPAN, wide), 0)
    for vt in vts:
        vt[DH:, :] = jnp.ones((vt.shape[0] - DH, vt.shape[1]), jnp.bfloat16)
    for copy in local[2:]:
        copy.wait()
    mine = []
    for p in range(count):
        copy = pltpu.make_async_copy(piece_of(p), bufs[p].at[me], own_sem.at[5 + p])
        copy.start()
        mine.append(copy)

    order = [me, sibling]
    for d in range(1, chips):
        order += [behind(d, core), behind(d, 1 - core)]
    for i in range(spans):
        here = table_ref[me * spans + i]
        for d, device in enumerate(order):
            for t in range(spans):
                there = table_ref[device * spans + t]
                bias[(i * n + d) * spans + t] = jnp.where(there < here, 0.0, HIDE)

    class Chunk:
        def __init__(self, parts, rows, base, vt, diagonal):
            self.parts = parts
            self.rows = rows
            self.base = base
            self.vt = vt
            self.diagonal = diagonal
            self.blocks = len(parts) * spans
            self.size = self.blocks * rows

        def stage(self):
            other = [part(1, t) for part in self.parts for t in range(spans)]
            self.vt[:DH, : self.size] = jnp.concatenate(other, axis=0).T

        def keys(self):
            return jnp.concatenate(
                [part(0, t) for part in self.parts for t in range(spans)], axis=0
            )

        def shift(self, i, t):
            if self.diagonal and t == i:
                return None
            return bias[i * n * spans + self.base * spans + t]

    def pair_of(u, i):
        return (u - i) // spans if isinstance(u, int) else lax.div(u - i, spans)

    def score(chunk, u, i, s):
        g = pair_of(u, i)
        keys = chunk.keys()
        value = jnp.concatenate(
            [
                lax.dot_general(
                    keys,
                    q_ref[
                        pl.ds(i * SPAN, SPAN),
                        pl.ds(pl.multiple_of((g * PAIR + h) * DH, DH), DH),
                    ],
                    (((1,), (1,)), ((), ())),
                    preferred_element_type=jnp.float32,
                )
                for h in range(PAIR)
            ],
            axis=1,
        )
        best = None
        rows = chunk.rows
        for t in range(chunk.blocks):
            part = value[t * rows : (t + 1) * rows]
            offset = chunk.shift(i, t)
            if offset is None:
                part = jnp.where(keys_at > rows_at, HIDE, part)
            s[t * rows : (t + 1) * rows] = part
            high = part[:8]
            for r in range(1, rows // 8):
                high = jnp.maximum(high, part[r * 8 : (r + 1) * 8])
            if offset is not None:
                high = high + offset
            best = high if best is None else jnp.maximum(best, high)
        best = jnp.broadcast_to(jnp.max(best, axis=0, keepdims=True), (8, wide))
        if chunk.diagonal:
            tops[u] = best
            return best, best
        old = tops[u]
        new = jnp.maximum(old, best)
        tops[u] = new
        return new, jnp.exp2((old - new) * rate)

    def weigh(chunk, i, high, s, w):
        rows = chunk.rows
        for t in range(chunk.blocks):
            offset = chunk.shift(i, t)
            level = high if offset is None else high - offset
            level = jnp.concatenate([level] * (rows // 8), axis=0)
            w[t * rows : (t + 1) * rows] = jnp.exp2(
                (s[t * rows : (t + 1) * rows] - level) * rate
            ).astype(jnp.bfloat16)

    def gather(chunk, u, factor, w):
        update = jnp.dot(
            chunk.vt[:, : chunk.size], w[: chunk.size], preferred_element_type=jnp.float32
        )
        update = update[: DH + 8]
        if not chunk.diagonal:
            update = acc[u] * jnp.concatenate([factor] * (DH // 8 + 1), axis=0) + update
        acc[u] = update
        return update

    def finish_unit(u, i, value):
        g = pair_of(u, i)
        share = 1.0 / value[DH : DH + 8]
        value = (value[:DH] * jnp.concatenate([share] * (DH // 8), axis=0)).T
        for h in range(PAIR):
            att[
                pl.ds(i * SPAN, SPAN), pl.ds(pl.multiple_of((g * PAIR + h) * DH, DH), DH)
            ] = value[h * SPAN : (h + 1) * SPAN].astype(jnp.bfloat16)

    ss, ww = (s0, s1), (p0, p1)

    def steps_of(chunk):
        most = min(pairs // 2, max(1, 8 * 512 // (spans * chunk.size)))
        return max(k for k in range(1, most + 1) if pairs % k == 0) * spans

    def attend(group, early, between, final):
        per = steps_of(group[0])
        turns = units // per

        def turn(j, carry, c, head, tail):
            chunk = group[c]
            (high, factor), late = carry
            for x in range(per):
                u = per * j + x
                now = x % 2
                weigh(chunk, x % spans, high, ss[now], ww[now])
                if x < per - 1 or not tail:
                    after = score(chunk, u + 1, (x + 1) % spans, ss[1 - now])
                elif c + 1 < len(group):
                    after = score(group[c + 1], 0, 0, ss[1 - now])
                else:
                    after = (high, factor)
                if x or not head:
                    value = gather(chunk, u - 1, late, ww[1 - now])
                    if x and final and c == len(group) - 1:
                        finish_unit(u - 1, (x - 1) % spans, value)
                elif c:
                    gather(group[c - 1], units - 1, late, ww[1 - now])
                late = factor
                high, factor = after
            return (high, factor), late

        group[0].stage()
        start = score(group[0], 0, 0, s0)
        carry = start, start[1]
        for c in range(len(group)):
            early(c)
            if turns > 1:
                carry = turn(0, carry, c, True, False)
                if turns > 2:
                    carry = lax.fori_loop(
                        1,
                        turns - 1,
                        lambda j, carry, c=c: turn(j, carry, c, False, False),
                        carry,
                    )
            between(c)
            if c + 1 < len(group):
                group[c + 1].stage()
            carry = turn(turns - 1, carry, c, turns == 1, True)
        value = gather(group[-1], units - 1, carry[1], ww[(per - 1) % 2])
        if final:
            finish_unit(units - 1, spans - 1, value)

            for j in range(turns - 1):
                u = per * j + per - 1
                finish_unit(u, spans - 1, acc[u])

    def idle(c):
        pass

    def spread_some(k):
        for p in range(1, count):
            if min(p, 3) == k:
                spread(p)

    attend(
        [Chunk([lambda j, t: own[j, t]], SPAN, 0, vts[0], True)],
        idle, lambda c: spread_some(1), False,
    )
    spread_some(2)

    wanted = []
    for s in range(spans):
        device, place = jnp.int32(0), jnp.int32(0)
        for g in range(n * spans):
            hit = slots_ref[g] == me * spans + s
            device = jnp.where(hit, g // spans, device)
            place = jnp.where(hit, g % spans, place)
        wanted.append((device, place))

    def relay(p):
        for d in range(1, chips):
            origin = behind(d, core)
            await_piece(p, origin, d)
            remote(p, bufs[p].at[origin], origin, chips, sibling).start()

    def complete(p):
        several(bufs[p], chips - 1, None, recv.at[p, chips]).wait_recv()
        select(p)
        if p < count - 1:
            publish(p)

    def page_copy(p, target, origin):
        ref = zbufs[p].at[origin]
        return pltpu.make_async_remote_copy(
            src_ref=ref,
            dst_ref=ref,
            send_sem=page_send.at[p],
            recv_sem=page_recv.at[p],
            device_id={"page": target},
            device_id_type=MESH,
        )

    def select(p):
        for s in range(spans):
            device, place = wanted[s]
            for j in range(2):
                zbufs[p][page, j, s] = bufs[p][device, j, place]

    def publish(p):
        for index in range(1, n_page):
            page_copy(p, (page + index) % n_page, page).start()

    def foreign(index, owner, target):
        ref = fbuf.at[owner]
        return pltpu.make_async_remote_copy(
            src_ref=ref,
            dst_ref=ref,
            send_sem=far_send.at[0],
            recv_sem=far_recv.at[index],
            device_id={"ctx": target},
            device_id_type=MESH,
        )

    def foreign_spread():
        several(zbufs[count - 1], n_page - 1, None, page_recv.at[count - 1]).wait_recv()
        for d in range(1, chips):
            foreign(d, me, ahead(d)).start()
        foreign(0, me, sibling).start()

    def foreign_relay():
        for d in range(1, chips):
            origin = behind(d, core)
            foreign(d, origin, sibling).wait_recv()
            foreign(chips, origin, sibling).start()

    def foreign_complete():
        foreign(0, sibling, sibling).wait_recv()
        several(fbuf, chips - 1, None, far_recv.at[chips]).wait_recv()
        for s in range(spans):
            device, place = wanted[s]
            for k in range(1, n_page):
                for j in range(2):
                    zbufs[count - 1][(page + k) % n_page, j, s] = fbuf[device, k - 1, j, place]

    for p in range(count):
        mine[p].wait()
        await_piece(p, sibling, 0)

    def beside(j, t):
        return jnp.concatenate([bufs[p][sibling, j, t] for p in range(count)], axis=0)

    def meet(c):
        spread_some(3)
        relay(0)

    attend([Chunk([beside], SPAN, 1, vts[0], False)], idle, meet, False)

    complete(0)
    def rows_of(some, device):
        return lambda j, t: jnp.concatenate([bufs[p][device, j, t] for p in some], axis=0)

    group = [
        Chunk(
            [rows_of(some, device) for device in order[2:]],
            sum(PIECES[p] for p in some), 2, vts[c % 2], False,
        )
        for c, some in enumerate(CHUNKS)
    ]

    def early(c):
        if c == 0:
            relay(1)
        elif c == 1:
            complete(2)
            relay(3)

    def between(c):
        if c == 0:
            complete(1)
            foreign_spread()
            relay(2)
        elif c == 1:
            complete(3)
        else:
            foreign_relay()

    attend(group, early, between, True)
    foreign_complete()

    finish = pltpu.make_async_copy(att, att_out, out_sem.at[0])
    finish.start()

    for p in range(count - 1):
        several(zbufs[p], n_page - 1, None, page_recv.at[p]).wait_recv()

    lanes = lax.broadcasted_iota(jnp.int32, (8, DH), 1)
    for s in range(spans):
        for j in range(2):
            levels = jnp.zeros((8, DH), jnp.float32)
            for h in range(n_page):
                level = None
                for p in range(count):
                    high = jnp.max(jnp.abs(zbufs[p][h, j, s].astype(jnp.float32)), axis=0, keepdims=True)
                    level = high if level is None else jnp.maximum(level, high)
                level = jnp.max(level, axis=1, keepdims=True) + 1e-06
                share = 1.0 / level
                for p in range(count):
                    cache[s, h, j, starts[p] : starts[p] + PIECES[p]] = (
                        zbufs[p][h, j, s].astype(jnp.float32) * share
                    ).astype(jnp.bfloat16)
                levels = jnp.where(lanes == h, level, levels)
            scales[s, j] = levels
    last = [
        pltpu.make_async_copy(cache, cache_out, out_sem.at[1]),
        pltpu.make_async_copy(scales, scales_out, out_sem.at[2]),
    ]
    for copy in last:
        copy.start()
    for p in range(count):
        several(bufs[p], n - 1, send.at[p], None).wait_send()
        several(zbufs[p], n_page - 1, page_send.at[p], None).wait_send()
    several(fbuf, n - 1, far_send.at[0], None).wait_send()
    finish.wait()
    for copy in last:
        copy.wait()


def place_results(att_in, cache_in, scales_in, att_out, cache_out, scales_out, sems):
    parts = sems.shape[0] - cache_in.shape[0]
    rows = att_in.shape[0] // parts
    moves = [
        (att_in.at[pl.ds(j * rows, rows)], att_out.at[pl.ds(j * rows, rows)]) for j in range(parts)
    ]
    moves += [(cache_in.at[s], cache_out.at[s]) for s in range(cache_in.shape[0])]
    moves = [pltpu.make_async_copy(*pair, sems.at[j]) for j, pair in enumerate(moves)]
    for copy in moves:
        copy.start()
    for s in range(scales_out.shape[0]):
        for j in range(scales_out.shape[1]):
            scales_out[s, j : j + 1] = scales_in[s, j, :1, : scales_out.shape[2]]
    for copy in moves:
        copy.wait()


def on_device(n, n_page, queries, keys, values, span_table, page_slots):
    rows = queries.shape[0]
    heads = queries.shape[1] // DH
    spans = rows // SPAN
    units = heads // PAIR * spans
    wide = PAIR * SPAN
    rows_most = max(sum(PIECES[p] for p in some) for some in CHUNKS)
    most = max(spans * SPAN, (n - 2) * spans * rows_most)
    padded = -(-most // 128) * 128
    any_space = pl.BlockSpec(memory_space=pl.ANY)
    vmem = pl.BlockSpec(memory_space=pltpu.VMEM)
    hbm = pl.BlockSpec(memory_space=pltpu.HBM)
    count = len(PIECES)
    results = (
        jax.ShapeDtypeStruct((rows, heads * DH), jnp.bfloat16),
        jax.ShapeDtypeStruct((spans, n_page, 2, PAGE, DH), jnp.bfloat16),
        jax.ShapeDtypeStruct((spans, 2, 8, DH), jnp.float32),
    )
    attended, cache, scales = pl.pallas_call(
        functools.partial(kernel, n, n_page, heads, spans),
        out_shape=results,
        in_specs=[hbm] * 5,
        out_specs=(any_space,) * 3,
        scratch_shapes=[
            pltpu.SMEM(span_table.shape, jnp.int32),
            pltpu.SMEM(page_slots.shape, jnp.int32),
            pltpu.SMEM((spans * n * spans,), jnp.float32),
            pltpu.VMEM(queries.shape, jnp.bfloat16),
            pltpu.VMEM((2, spans, SPAN, DH), jnp.bfloat16),
            [pltpu.VMEM((DH + 16, padded), jnp.bfloat16)] * 2,
            pltpu.VMEM((most, wide), jnp.float32),
            pltpu.VMEM((most, wide), jnp.float32),
            pltpu.VMEM((most, wide), jnp.bfloat16),
            pltpu.VMEM((most, wide), jnp.bfloat16),
            pltpu.VMEM((units, 8, wide), jnp.float32),
            pltpu.VMEM((units, DH + 8, wide), jnp.float32),
            pltpu.VMEM(queries.shape, jnp.bfloat16),
            pltpu.VMEM((spans, n_page, 2, PAGE, DH), jnp.bfloat16),
            pltpu.VMEM((spans, 2, 8, DH), jnp.float32),
            pltpu.SemaphoreType.DMA((count,)),
            pltpu.SemaphoreType.DMA((count, n // 2 + 1)),
            pltpu.SemaphoreType.DMA((5 + count,)),
            pltpu.SemaphoreType.DMA((count,)),
            pltpu.SemaphoreType.DMA((count,)),
            pltpu.SemaphoreType.DMA((1,)),
            pltpu.SemaphoreType.DMA((n // 2 + 1,)),
            pltpu.SemaphoreType.DMA((3,)),
            pltpu.VMEM((n, n_page - 1, 2, spans, PIECES[-1], DH), jnp.bfloat16),
        ]
        + [pltpu.VMEM((n, 2, spans, p, DH), jnp.bfloat16) for p in PIECES]
        + [pltpu.VMEM((n_page, 2, spans, p, DH), jnp.bfloat16) for p in PIECES],
        compiler_params=pltpu.CompilerParams(
            collective_id=0, has_side_effects=True, vmem_limit_bytes=48 * 2**20
        ),
    )(
        *(
            pltpu.with_memory_space_constraint(x, pltpu.HBM)
            for x in (
                span_table,
                page_slots,
                queries,
                keys.reshape(spans, SPAN, DH),
                values.reshape(spans, SPAN, DH),
            )
        )
    )
    attended, cache, scales = pl.pallas_call(
        place_results,
        out_shape=results[:2] + (jax.ShapeDtypeStruct((spans, 2, n_page), jnp.float32),),
        in_specs=[any_space, any_space, vmem],
        out_specs=(any_space, any_space, vmem),
        scratch_shapes=[
            pltpu.SemaphoreType.DMA((4 + spans,)),
        ],
        compiler_params=pltpu.CompilerParams(vmem_limit_bytes=16 * 2**20),
    )(attended, cache, scales)
    return attended, cache, scales.transpose(0, 2, 1)


def solution(mesh):
    placed = (P("ctx", "page"), P("ctx", "page"), P("ctx", "page"), P(), P())
    return jax.shard_map(
        functools.partial(on_device, mesh.shape["ctx"], mesh.shape["page"]),
        mesh=mesh,
        in_specs=placed,
        out_specs=(P("ctx", "page"), P("ctx", None, None, None, None), P("ctx", None, None)),
        check_vma=False,
    )
```

```python
import functools
import math

import jax
import jax.numpy as jnp
from jax import lax
from jax.experimental import pallas as pl
from jax.experimental.pallas import tpu as pltpu
from jax.sharding import PartitionSpec as P

DH = 128
PAGE = 128
SPAN = 128
HIDE = -1e30
PAIR = 2
PIECES = (32, 32, 32, 32)
CHUNKS = ((0,), (1,), (2, 3))
HANDED = (0,)
MESH = pl.DeviceIdType.MESH


def kernel(
    n, n_page, heads, spans, table_in, slots_in, q_in, k_in, v_in,
    att_out, cache_out, scales_out,
    table_ref, slots_ref, bias, q_ref, own, vts, s0, s1, p0, p1,
    tops, acc, att, cache, scales, send, recv, own_sem, page_send, page_recv, far_send, far_recv, out_sem, fbuf,
    *pieces,
):
    count = len(PIECES)
    bufs, zbufs = pieces[:count], pieces[count:]
    starts = [sum(PIECES[:p]) for p in range(count)]
    chips = n // 2
    pairs = heads // PAIR
    wide = PAIR * SPAN
    units = pairs * spans
    me = lax.axis_index("ctx")
    page = lax.axis_index("page")
    chip = me // 2
    core = me % 2
    sibling = 2 * chip + 1 - core
    rate = DH ** (-0.5) * math.log2(math.e)

    def ahead(d):
        return 2 * ((chip + d) % chips) + core

    def behind(d, c):
        return 2 * ((chip + chips - d) % chips) + c

    barrier = pltpu.get_barrier_semaphore()
    for d in range(1, chips):
        pl.semaphore_signal(barrier, inc=1, device_id={"ctx": ahead(d)}, device_id_type=MESH)
    pl.semaphore_signal(barrier, inc=1, device_id={"ctx": sibling}, device_id_type=MESH)
    for d in range(1, n_page):
        pl.semaphore_signal(
            barrier, inc=1, device_id={"page": (page + d) % n_page}, device_id_type=MESH
        )

    local = []

    def fetch(src, dst, j):
        copy = pltpu.make_async_copy(src, dst, own_sem.at[j])
        copy.start()
        local.append(copy)

    fetch(k_in, own.at[0], 0)
    fetch(v_in, own.at[1], 1)
    fetch(table_in, table_ref, 2)
    fetch(q_in, q_ref, 3)
    fetch(slots_in, slots_ref, 4)

    pl.semaphore_wait(barrier, chips + n_page - 1)

    def remote(p, src, owner, index, target):
        return pltpu.make_async_remote_copy(
            src_ref=src,
            dst_ref=bufs[p].at[owner],
            send_sem=send.at[p],
            recv_sem=recv.at[p, index],
            device_id={"ctx": target},
            device_id_type=MESH,
        )

    def several(ref, copies, send_sem, recv_sem):
        some = ref.at[pl.ds(0, copies)]
        return pltpu.make_async_remote_copy(
            src_ref=some,
            dst_ref=some,
            send_sem=recv_sem if send_sem is None else send_sem,
            recv_sem=send_sem if recv_sem is None else recv_sem,
            device_id={"ctx": sibling},
            device_id_type=MESH,
        )

    def await_piece(p, owner, index):
        remote(p, bufs[p].at[owner], owner, index, sibling).wait_recv()

    def piece_of(p):
        return own.at[:, :, pl.ds(starts[p], PIECES[p])]

    def spread(p):
        for d in range(1, chips):
            remote(p, piece_of(p), me, d, ahead(d)).start()

    def across(index):
        return pltpu.make_async_remote_copy(
            src_ref=piece_of(count - 1),
            dst_ref=fbuf.at[me, n_page - index - 1],
            send_sem=page_send.at[count - 1],
            recv_sem=page_recv.at[count - 1],
            device_id={"page": (page + index) % n_page},
            device_id_type=MESH,
        )

    for copy in local[:2]:
        copy.wait()
    spread(0)
    for index in range(1, n_page):
        across(index).start()
    for p in range(count):
        remote(p, piece_of(p), me, 0, sibling).start()

    rows_at = lax.broadcasted_iota(jnp.int32, (SPAN, wide), 1) % SPAN
    keys_at = lax.broadcasted_iota(jnp.int32, (SPAN, wide), 0)
    for vt in vts:
        vt[DH:, :] = jnp.ones((vt.shape[0] - DH, vt.shape[1]), jnp.bfloat16)
    for copy in local[2:]:
        copy.wait()
    mine = []
    for p in range(count):
        copy = pltpu.make_async_copy(piece_of(p), bufs[p].at[me], own_sem.at[5 + p])
        copy.start()
        mine.append(copy)

    order = [me, sibling]
    for d in range(1, chips):
        order += [behind(d, core), behind(d, 1 - core)]
    for i in range(spans):
        here = table_ref[me * spans + i]
        for d, device in enumerate(order):
            for t in range(spans):
                there = table_ref[device * spans + t]
                bias[(i * n + d) * spans + t] = jnp.where(there < here, 0.0, HIDE)

    class Chunk:
        def __init__(self, parts, rows, base, vt, diagonal):
            self.parts = parts
            self.rows = rows
            self.base = base
            self.vt = vt
            self.diagonal = diagonal
            self.blocks = len(parts) * spans
            self.size = self.blocks * rows

        def stage(self):
            other = [part(1, t) for part in self.parts for t in range(spans)]
            self.vt[:DH, : self.size] = jnp.concatenate(other, axis=0).T

        def keys(self):
            return jnp.concatenate(
                [part(0, t) for part in self.parts for t in range(spans)], axis=0
            )

        def shift(self, i, t):
            if self.diagonal and t == i:
                return None
            return bias[i * n * spans + self.base * spans + t]

    def pair_of(u, i):
        return (u - i) // spans if isinstance(u, int) else lax.div(u - i, spans)

    def score(chunk, u, i, s):
        g = pair_of(u, i)
        keys = chunk.keys()
        value = jnp.concatenate(
            [
                lax.dot_general(
                    keys,
                    q_ref[
                        pl.ds(i * SPAN, SPAN),
                        pl.ds(pl.multiple_of((g * PAIR + h) * DH, DH), DH),
                    ],
                    (((1,), (1,)), ((), ())),
                    preferred_element_type=jnp.float32,
                )
                for h in range(PAIR)
            ],
            axis=1,
        )
        best = None
        rows = chunk.rows
        for t in range(chunk.blocks):
            part = value[t * rows : (t + 1) * rows]
            offset = chunk.shift(i, t)
            if offset is None:
                part = jnp.where(keys_at > rows_at, HIDE, part)
            s[t * rows : (t + 1) * rows] = part
            high = part[:8]
            for r in range(1, rows // 8):
                high = jnp.maximum(high, part[r * 8 : (r + 1) * 8])
            if offset is not None:
                high = high + offset
            best = high if best is None else jnp.maximum(best, high)
        best = jnp.broadcast_to(jnp.max(best, axis=0, keepdims=True), (8, wide))
        if chunk.diagonal:
            tops[u] = best
            return best, best
        old = tops[u]
        new = jnp.maximum(old, best)
        tops[u] = new
        return new, jnp.exp2((old - new) * rate)

    def weigh(chunk, i, high, s, w):
        rows = chunk.rows
        for t in range(chunk.blocks):
            offset = chunk.shift(i, t)
            level = high if offset is None else high - offset
            level = jnp.concatenate([level] * (rows // 8), axis=0)
            w[t * rows : (t + 1) * rows] = jnp.exp2(
                (s[t * rows : (t + 1) * rows] - level) * rate
            ).astype(jnp.bfloat16)

    def gather(chunk, u, factor, w):
        update = jnp.dot(
            chunk.vt[:, : chunk.size], w[: chunk.size], preferred_element_type=jnp.float32
        )
        update = update[: DH + 8]
        if not chunk.diagonal:
            update = acc[u] * jnp.concatenate([factor] * (DH // 8 + 1), axis=0) + update
        acc[u] = update
        return update

    def finish_unit(u, i, value):
        g = pair_of(u, i)
        share = 1.0 / value[DH : DH + 8]
        value = (value[:DH] * jnp.concatenate([share] * (DH // 8), axis=0)).T
        for h in range(PAIR):
            att[
                pl.ds(i * SPAN, SPAN), pl.ds(pl.multiple_of((g * PAIR + h) * DH, DH), DH)
            ] = value[h * SPAN : (h + 1) * SPAN].astype(jnp.bfloat16)

    ss, ww = (s0, s1), (p0, p1)

    def steps_of(chunk):
        most = min(pairs // 2, max(1, 8 * 512 // (spans * chunk.size)))
        return max(k for k in range(1, most + 1) if pairs % k == 0) * spans

    def attend(group, early, between, final):
        per = steps_of(group[0])
        turns = units // per

        def turn(j, carry, c, head, tail):
            chunk = group[c]
            (high, factor), late = carry
            for x in range(per):
                u = per * j + x
                now = x % 2
                weigh(chunk, x % spans, high, ss[now], ww[now])
                if x < per - 1 or not tail:
                    after = score(chunk, u + 1, (x + 1) % spans, ss[1 - now])
                elif c + 1 < len(group):
                    after = score(group[c + 1], 0, 0, ss[1 - now])
                else:
                    after = (high, factor)
                if x or not head:
                    value = gather(chunk, u - 1, late, ww[1 - now])
                    if x and final and c == len(group) - 1:
                        finish_unit(u - 1, (x - 1) % spans, value)
                elif c:
                    gather(group[c - 1], units - 1, late, ww[1 - now])
                late = factor
                high, factor = after
            return (high, factor), late

        group[0].stage()
        start = score(group[0], 0, 0, s0)
        carry = start, start[1]
        for c in range(len(group)):
            early(c)
            if turns > 1:
                carry = turn(0, carry, c, True, False)
                if turns > 2:
                    carry = lax.fori_loop(
                        1,
                        turns - 1,
                        lambda j, carry, c=c: turn(j, carry, c, False, False),
                        carry,
                    )
            between(c)
            if c + 1 < len(group):
                group[c + 1].stage()
            carry = turn(turns - 1, carry, c, turns == 1, True)
        value = gather(group[-1], units - 1, carry[1], ww[(per - 1) % 2])
        if final:
            finish_unit(units - 1, spans - 1, value)

            for j in range(turns - 1):
                u = per * j + per - 1
                finish_unit(u, spans - 1, acc[u])

    def idle(c):
        pass

    def spread_some(k):
        for p in range(1, count):
            if min(p, 3) == k:
                spread(p)

    attend(
        [Chunk([lambda j, t: own[j, t]], SPAN, 0, vts[0], True)],
        idle, lambda c: spread_some(1), False,
    )
    spread_some(2)

    wanted = []
    for s in range(spans):
        device, place = jnp.int32(0), jnp.int32(0)
        for g in range(n * spans):
            hit = slots_ref[g] == me * spans + s
            device = jnp.where(hit, g // spans, device)
            place = jnp.where(hit, g % spans, place)
        wanted.append((device, place))

    def relay(p):
        for d in range(1, chips):
            origin = behind(d, core)
            await_piece(p, origin, d)
            remote(p, bufs[p].at[origin], origin, chips, sibling).start()

    def complete(p):
        several(bufs[p], chips - 1, None, recv.at[p, chips]).wait_recv()
        select(p)
        if p < count - 1:
            publish(p)

    def page_copy(p, target, origin, held=False):
        ref = zbufs[p].at[origin]
        return pltpu.make_async_remote_copy(
            src_ref=ref,
            dst_ref=ref,
            send_sem=page_send.at[p],
            recv_sem=page_recv.at[count + p if held else p],
            device_id={"page": target},
            device_id_type=MESH,
        )

    def within(place):
        return jnp.logical_and(place >= 0, place < n_page)

    def handed(p):
        return n_page == 4 and p in HANDED

    inner = jnp.logical_and(page > 0, page < n_page - 1)

    def select(p):
        for s in range(spans):
            device, place = wanted[s]
            for j in range(2):
                zbufs[p][page, j, s] = bufs[p][device, j, place]

    def publish(p):
        if not handed(p):
            for index in range(1, n_page):
                page_copy(p, (page + index) % n_page, page).start()
            return
        for sign in (-1, 1):
            @pl.when(within(page + sign))
            def _(sign=sign):
                page_copy(p, page + sign, page).start()

            @pl.when(within(page + 3 * sign))
            def _(sign=sign):
                page_copy(p, page + 2 * sign, page, True).start()

            @pl.when(jnp.logical_and(within(page + 2 * sign), inner))
            def _(sign=sign):
                page_copy(p, page + 2 * sign, page).start()

    def hand_on(p):
        if handed(p):
            for sign in (-1, 1):
                @pl.when(jnp.logical_and(within(page - 2 * sign), inner))
                def _(sign=sign):
                    page_copy(p, page + sign, page - 2 * sign, True).wait_recv()
                    page_copy(p, page + sign, page - 2 * sign).start()

    def each_amount(p, outer_count, inner_count, action):
        if not handed(p):
            action(n_page - 1)
            return

        @pl.when(inner)
        def _():
            action(inner_count)

        @pl.when(jnp.logical_not(inner))
        def _():
            action(outer_count)

    def foreign(index, owner, target):
        ref = fbuf.at[owner]
        return pltpu.make_async_remote_copy(
            src_ref=ref,
            dst_ref=ref,
            send_sem=far_send.at[0],
            recv_sem=far_recv.at[index],
            device_id={"ctx": target},
            device_id_type=MESH,
        )

    def foreign_spread():
        several(zbufs[count - 1], n_page - 1, None, page_recv.at[count - 1]).wait_recv()
        for d in range(1, chips):
            foreign(d, me, ahead(d)).start()
        foreign(0, me, sibling).start()

    def foreign_relay():
        for d in range(1, chips):
            origin = behind(d, core)
            foreign(d, origin, sibling).wait_recv()
            foreign(chips, origin, sibling).start()

    def foreign_complete():
        foreign(0, sibling, sibling).wait_recv()
        several(fbuf, chips - 1, None, far_recv.at[chips]).wait_recv()
        for s in range(spans):
            device, place = wanted[s]
            for k in range(1, n_page):
                for j in range(2):
                    zbufs[count - 1][(page + k) % n_page, j, s] = fbuf[device, k - 1, j, place]

    for p in range(count):
        mine[p].wait()
        await_piece(p, sibling, 0)

    def beside(j, t):
        return jnp.concatenate([bufs[p][sibling, j, t] for p in range(count)], axis=0)

    def meet(c):
        spread_some(3)
        relay(0)

    attend([Chunk([beside], SPAN, 1, vts[0], False)], idle, meet, False)

    complete(0)
    def rows_of(some, device):
        return lambda j, t: jnp.concatenate([bufs[p][device, j, t] for p in some], axis=0)

    group = [
        Chunk(
            [rows_of(some, device) for device in order[2:]],
            sum(PIECES[p] for p in some), 2, vts[c % 2], False,
        )
        for c, some in enumerate(CHUNKS)
    ]

    def early(c):
        if c == 0:
            foreign_spread()
            relay(1)
        elif c == 1:
            complete(2)
            relay(3)

    def between(c):
        if c == 0:
            complete(1)
            relay(2)
        elif c == 1:
            complete(3)
            hand_on(0)
        else:
            foreign_relay()
            hand_on(1)

    attend(group, early, between, True)
    foreign_complete()

    finish = pltpu.make_async_copy(att, att_out, out_sem.at[0])
    finish.start()

    for p in range(count - 1):
        each_amount(
            p, 3, 2, lambda k, p=p: several(zbufs[p], k, None, page_recv.at[p]).wait_recv()
        )

    lanes = lax.broadcasted_iota(jnp.int32, (8, DH), 1)
    for s in range(spans):
        for j in range(2):
            levels = jnp.zeros((8, DH), jnp.float32)
            for h in range(n_page):
                level = None
                for p in range(count):
                    high = jnp.max(jnp.abs(zbufs[p][h, j, s].astype(jnp.float32)), axis=0, keepdims=True)
                    level = high if level is None else jnp.maximum(level, high)
                level = jnp.max(level, axis=1, keepdims=True) + 1e-06
                share = 1.0 / level
                for p in range(count):
                    cache[s, h, j, starts[p] : starts[p] + PIECES[p]] = (
                        zbufs[p][h, j, s].astype(jnp.float32) * share
                    ).astype(jnp.bfloat16)
                levels = jnp.where(lanes == h, level, levels)
            scales[s, j] = levels
    last = [
        pltpu.make_async_copy(cache, cache_out, out_sem.at[1]),
        pltpu.make_async_copy(scales, scales_out, out_sem.at[2]),
    ]
    for copy in last:
        copy.start()
    for p in range(count):
        several(bufs[p], n - 1, send.at[p], None).wait_send()
        each_amount(
            p, 2, 4, lambda k, p=p: several(zbufs[p], k, page_send.at[p], None).wait_send()
        )
    several(fbuf, n - 1, far_send.at[0], None).wait_send()
    finish.wait()
    for copy in last:
        copy.wait()


def place_results(att_in, cache_in, scales_in, att_out, cache_out, scales_out, sems):
    parts = sems.shape[0] - cache_in.shape[0]
    rows = att_in.shape[0] // parts
    moves = [
        (att_in.at[pl.ds(j * rows, rows)], att_out.at[pl.ds(j * rows, rows)]) for j in range(parts)
    ]
    moves += [(cache_in.at[s], cache_out.at[s]) for s in range(cache_in.shape[0])]
    moves = [pltpu.make_async_copy(*pair, sems.at[j]) for j, pair in enumerate(moves)]
    for copy in moves:
        copy.start()
    for s in range(scales_out.shape[0]):
        for j in range(scales_out.shape[1]):
            scales_out[s, j : j + 1] = scales_in[s, j, :1, : scales_out.shape[2]]
    for copy in moves:
        copy.wait()


def on_device(n, n_page, queries, keys, values, span_table, page_slots):
    rows = queries.shape[0]
    heads = queries.shape[1] // DH
    spans = rows // SPAN
    units = heads // PAIR * spans
    wide = PAIR * SPAN
    rows_most = max(sum(PIECES[p] for p in some) for some in CHUNKS)
    most = max(spans * SPAN, (n - 2) * spans * rows_most)
    padded = -(-most // 128) * 128
    any_space = pl.BlockSpec(memory_space=pl.ANY)
    vmem = pl.BlockSpec(memory_space=pltpu.VMEM)
    hbm = pl.BlockSpec(memory_space=pltpu.HBM)
    count = len(PIECES)
    results = (
        jax.ShapeDtypeStruct((rows, heads * DH), jnp.bfloat16),
        jax.ShapeDtypeStruct((spans, n_page, 2, PAGE, DH), jnp.bfloat16),
        jax.ShapeDtypeStruct((spans, 2, 8, DH), jnp.float32),
    )
    attended, cache, scales = pl.pallas_call(
        functools.partial(kernel, n, n_page, heads, spans),
        out_shape=results,
        in_specs=[hbm] * 5,
        out_specs=(any_space,) * 3,
        scratch_shapes=[
            pltpu.SMEM(span_table.shape, jnp.int32),
            pltpu.SMEM(page_slots.shape, jnp.int32),
            pltpu.SMEM((spans * n * spans,), jnp.float32),
            pltpu.VMEM(queries.shape, jnp.bfloat16),
            pltpu.VMEM((2, spans, SPAN, DH), jnp.bfloat16),
            [pltpu.VMEM((DH + 16, padded), jnp.bfloat16)] * 2,
            pltpu.VMEM((most, wide), jnp.float32),
            pltpu.VMEM((most, wide), jnp.float32),
            pltpu.VMEM((most, wide), jnp.bfloat16),
            pltpu.VMEM((most, wide), jnp.bfloat16),
            pltpu.VMEM((units, 8, wide), jnp.float32),
            pltpu.VMEM((units, DH + 8, wide), jnp.float32),
            pltpu.VMEM(queries.shape, jnp.bfloat16),
            pltpu.VMEM((spans, n_page, 2, PAGE, DH), jnp.bfloat16),
            pltpu.VMEM((spans, 2, 8, DH), jnp.float32),
            pltpu.SemaphoreType.DMA((count,)),
            pltpu.SemaphoreType.DMA((count, n // 2 + 1)),
            pltpu.SemaphoreType.DMA((5 + count,)),
            pltpu.SemaphoreType.DMA((count,)),
            pltpu.SemaphoreType.DMA((count + len(HANDED),)),
            pltpu.SemaphoreType.DMA((1,)),
            pltpu.SemaphoreType.DMA((n // 2 + 1,)),
            pltpu.SemaphoreType.DMA((3,)),
            pltpu.VMEM((n, n_page - 1, 2, spans, PIECES[-1], DH), jnp.bfloat16),
        ]
        + [pltpu.VMEM((n, 2, spans, p, DH), jnp.bfloat16) for p in PIECES]
        + [pltpu.VMEM((n_page, 2, spans, p, DH), jnp.bfloat16) for p in PIECES],
        compiler_params=pltpu.CompilerParams(
            collective_id=0, has_side_effects=True, vmem_limit_bytes=48 * 2**20
        ),
    )(
        *(
            pltpu.with_memory_space_constraint(x, pltpu.HBM)
            for x in (
                span_table,
                page_slots,
                queries,
                keys.reshape(spans, SPAN, DH),
                values.reshape(spans, SPAN, DH),
            )
        )
    )
    attended, cache, scales = pl.pallas_call(
        place_results,
        out_shape=results[:2] + (jax.ShapeDtypeStruct((spans, 2, n_page), jnp.float32),),
        in_specs=[any_space, any_space, vmem],
        out_specs=(any_space, any_space, vmem),
        scratch_shapes=[
            pltpu.SemaphoreType.DMA((4 + spans,)),
        ],
        compiler_params=pltpu.CompilerParams(vmem_limit_bytes=16 * 2**20),
    )(attended, cache, scales)
    return attended, cache, scales.transpose(0, 2, 1)


def solution(mesh):
    placed = (P("ctx", "page"), P("ctx", "page"), P("ctx", "page"), P(), P())
    return jax.shard_map(
        functools.partial(on_device, mesh.shape["ctx"], mesh.shape["page"]),
        mesh=mesh,
        in_specs=placed,
        out_specs=(P("ctx", "page"), P("ctx", None, None, None, None), P("ctx", None, None)),
        check_vma=False,
    )
```

```python
import functools
import math

import jax
import jax.numpy as jnp
from jax import lax
from jax.experimental import pallas as pl
from jax.experimental.pallas import tpu as pltpu
from jax.sharding import PartitionSpec as P

DH = 128
PAGE = 128
SPAN = 128
HIDE = -1e30
PAIR = 2
PIECES = (32, 32, 32, 32)
CHUNKS = ((0,), (1,), (2, 3))
HANDED = (0, 1)
MESH = pl.DeviceIdType.MESH


def kernel(
    n, n_page, heads, spans, table_in, slots_in, q_in, k_in, v_in,
    att_out, cache_out, scales_out,
    table_ref, slots_ref, bias, q_ref, own, vts, s0, s1, p0, p1,
    tops, acc, att, cache, scales, send, recv, own_sem, page_send, page_recv, far_send, far_recv, out_sem, fbuf,
    *pieces,
):
    count = len(PIECES)
    bufs, zbufs = pieces[:count], pieces[count:]
    starts = [sum(PIECES[:p]) for p in range(count)]
    chips = n // 2
    pairs = heads // PAIR
    wide = PAIR * SPAN
    units = pairs * spans
    me = lax.axis_index("ctx")
    page = lax.axis_index("page")
    chip = me // 2
    core = me % 2
    sibling = 2 * chip + 1 - core
    rate = DH ** (-0.5) * math.log2(math.e)

    even = chips & (chips - 1) == 0

    def across_from(d, back):
        if not even:
            return (chip + chips - d) % chips if back else (chip + d) % chips
        place, bit = chip, 1
        while bit < chips:
            if d & bit:
                place = place + bit * (1 - 2 * (place // bit % 2))
            bit *= 2
        return place

    def ahead(d):
        return 2 * across_from(d, False) + core

    def behind(d, c):
        return 2 * across_from(d, True) + c

    barrier = pltpu.get_barrier_semaphore()
    for d in range(1, chips):
        pl.semaphore_signal(barrier, inc=1, device_id={"ctx": ahead(d)}, device_id_type=MESH)
    pl.semaphore_signal(barrier, inc=1, device_id={"ctx": sibling}, device_id_type=MESH)
    for d in range(1, n_page):
        pl.semaphore_signal(
            barrier, inc=1, device_id={"page": (page + d) % n_page}, device_id_type=MESH
        )

    local = []

    def fetch(src, dst, j):
        copy = pltpu.make_async_copy(src, dst, own_sem.at[j])
        copy.start()
        local.append(copy)

    fetch(k_in, own.at[0], 0)
    fetch(v_in, own.at[1], 1)
    fetch(table_in, table_ref, 2)
    fetch(q_in, q_ref, 3)
    fetch(slots_in, slots_ref, 4)

    pl.semaphore_wait(barrier, chips + n_page - 1)

    def remote(p, src, owner, index, target):
        return pltpu.make_async_remote_copy(
            src_ref=src,
            dst_ref=bufs[p].at[owner],
            send_sem=send.at[p],
            recv_sem=recv.at[p, index],
            device_id={"ctx": target},
            device_id_type=MESH,
        )

    def several(ref, copies, send_sem, recv_sem):
        some = ref.at[pl.ds(0, copies)]
        return pltpu.make_async_remote_copy(
            src_ref=some,
            dst_ref=some,
            send_sem=recv_sem if send_sem is None else send_sem,
            recv_sem=send_sem if recv_sem is None else recv_sem,
            device_id={"ctx": sibling},
            device_id_type=MESH,
        )

    def await_piece(p, owner, index):
        remote(p, bufs[p].at[owner], owner, index, sibling).wait_recv()

    def piece_of(p):
        return own.at[:, :, pl.ds(starts[p], PIECES[p])]

    def spread(p):
        for d in range(chips - 1, 0, -1):
            remote(p, piece_of(p), me, d, ahead(d)).start()

    def across(index):
        return pltpu.make_async_remote_copy(
            src_ref=piece_of(count - 1),
            dst_ref=fbuf.at[me, n_page - index - 1],
            send_sem=page_send.at[count - 1],
            recv_sem=page_recv.at[count - 1],
            device_id={"page": (page + index) % n_page},
            device_id_type=MESH,
        )

    for copy in local[:2]:
        copy.wait()
    spread(0)
    for index in range(1, n_page):
        across(index).start()
    for p in range(count):
        remote(p, piece_of(p), me, 0, sibling).start()

    rows_at = lax.broadcasted_iota(jnp.int32, (SPAN, wide), 1) % SPAN
    keys_at = lax.broadcasted_iota(jnp.int32, (SPAN, wide), 0)
    for vt in vts:
        vt[DH:, :] = jnp.ones((vt.shape[0] - DH, vt.shape[1]), jnp.bfloat16)
    for copy in local[2:]:
        copy.wait()
    mine = []
    for p in range(count):
        copy = pltpu.make_async_copy(piece_of(p), bufs[p].at[me], own_sem.at[5 + p])
        copy.start()
        mine.append(copy)

    order = [me, sibling]
    for d in range(1, chips):
        order += [behind(d, core), behind(d, 1 - core)]
    for i in range(spans):
        here = table_ref[me * spans + i]
        for d, device in enumerate(order):
            for t in range(spans):
                there = table_ref[device * spans + t]
                bias[(i * n + d) * spans + t] = jnp.where(there < here, 0.0, HIDE)

    class Chunk:
        def __init__(self, parts, rows, base, vt, diagonal):
            self.parts = parts
            self.rows = rows
            self.base = base
            self.vt = vt
            self.diagonal = diagonal
            self.blocks = len(parts) * spans
            self.size = self.blocks * rows

        def stage(self):
            other = [part(1, t) for part in self.parts for t in range(spans)]
            self.vt[:DH, : self.size] = jnp.concatenate(other, axis=0).T

        def keys(self):
            return jnp.concatenate(
                [part(0, t) for part in self.parts for t in range(spans)], axis=0
            )

        def shift(self, i, t):
            if self.diagonal and t == i:
                return None
            return bias[i * n * spans + self.base * spans + t]

    def pair_of(u, i):
        return (u - i) // spans if isinstance(u, int) else lax.div(u - i, spans)

    def score(chunk, u, i, s):
        g = pair_of(u, i)
        keys = chunk.keys()
        value = jnp.concatenate(
            [
                lax.dot_general(
                    keys,
                    q_ref[
                        pl.ds(i * SPAN, SPAN),
                        pl.ds(pl.multiple_of((g * PAIR + h) * DH, DH), DH),
                    ],
                    (((1,), (1,)), ((), ())),
                    preferred_element_type=jnp.float32,
                )
                for h in range(PAIR)
            ],
            axis=1,
        )
        best = None
        rows = chunk.rows
        for t in range(chunk.blocks):
            part = value[t * rows : (t + 1) * rows]
            offset = chunk.shift(i, t)
            if offset is None:
                part = jnp.where(keys_at > rows_at, HIDE, part)
            s[t * rows : (t + 1) * rows] = part
            high = part[:8]
            for r in range(1, rows // 8):
                high = jnp.maximum(high, part[r * 8 : (r + 1) * 8])
            if offset is not None:
                high = high + offset
            best = high if best is None else jnp.maximum(best, high)
        best = jnp.broadcast_to(jnp.max(best, axis=0, keepdims=True), (8, wide))
        if chunk.diagonal:
            tops[u] = best
            return best, best
        old = tops[u]
        new = jnp.maximum(old, best)
        tops[u] = new
        return new, jnp.exp2((old - new) * rate)

    def weigh(chunk, i, high, s, w):
        rows = chunk.rows
        for t in range(chunk.blocks):
            offset = chunk.shift(i, t)
            level = high if offset is None else high - offset
            level = jnp.concatenate([level] * (rows // 8), axis=0)
            w[t * rows : (t + 1) * rows] = jnp.exp2(
                (s[t * rows : (t + 1) * rows] - level) * rate
            ).astype(jnp.bfloat16)

    def gather(chunk, u, factor, w):
        update = jnp.dot(
            chunk.vt[:, : chunk.size], w[: chunk.size], preferred_element_type=jnp.float32
        )
        update = update[: DH + 8]
        if not chunk.diagonal:
            update = acc[u] * jnp.concatenate([factor] * (DH // 8 + 1), axis=0) + update
        acc[u] = update
        return update

    def finish_unit(u, i, value):
        g = pair_of(u, i)
        share = 1.0 / value[DH : DH + 8]
        value = (value[:DH] * jnp.concatenate([share] * (DH // 8), axis=0)).T
        for h in range(PAIR):
            att[
                pl.ds(i * SPAN, SPAN), pl.ds(pl.multiple_of((g * PAIR + h) * DH, DH), DH)
            ] = value[h * SPAN : (h + 1) * SPAN].astype(jnp.bfloat16)

    ss, ww = (s0, s1), (p0, p1)

    def steps_of(chunk):
        most = min(pairs // 2, max(1, 8 * 512 // (spans * chunk.size)))
        return max(k for k in range(1, most + 1) if pairs % k == 0) * spans

    def attend(group, early, middle, between, final):
        pers = [steps_of(chunk) for chunk in group]

        def turn(j, carry, c, head, tail):
            chunk, per = group[c], pers[c]
            (high, factor), late = carry
            for x in range(per):
                u = per * j + x
                now = x % 2
                weigh(chunk, x % spans, high, ss[now], ww[now])
                if x < per - 1 or not tail:
                    after = score(chunk, u + 1, (x + 1) % spans, ss[1 - now])
                elif c + 1 < len(group):
                    after = score(group[c + 1], 0, 0, ss[1 - now])
                else:
                    after = (high, factor)
                if x or not head:
                    value = gather(chunk, u - 1, late, ww[1 - now])
                    if x and final and c == len(group) - 1:
                        finish_unit(u - 1, (x - 1) % spans, value)
                elif c:
                    gather(group[c - 1], units - 1, late, ww[1 - now])
                late = factor
                high, factor = after
            return (high, factor), late

        group[0].stage()
        start = score(group[0], 0, 0, s0)
        carry = start, start[1]
        for c in range(len(group)):
            turns = units // pers[c]
            early(c)
            if turns > 1:
                carry = turn(0, carry, c, True, False)
                half = turns // 2
                for part, (low, high) in enumerate(((1, half), (half, turns - 1))):
                    if part:
                        middle(c)
                    if low < high:
                        carry = lax.fori_loop(
                            low,
                            high,
                            lambda j, carry, c=c: turn(j, carry, c, False, False),
                            carry,
                        )
            else:
                middle(c)
            between(c)
            if c + 1 < len(group):
                group[c + 1].stage()
            carry = turn(turns - 1, carry, c, turns == 1, True)
        per = pers[-1]
        value = gather(group[-1], units - 1, carry[1], ww[(per - 1) % 2])
        if final:
            finish_unit(units - 1, spans - 1, value)

            for j in range(units // per - 1):
                u = per * j + per - 1
                finish_unit(u, spans - 1, acc[u])

    def idle(c):
        pass

    def spread_some(k):
        for p in range(1, count):
            if min(p, 3) == k:
                spread(p)

    attend(
        [Chunk([lambda j, t: own[j, t]], SPAN, 0, vts[0], True)],
        idle, idle, lambda c: spread_some(1), False,
    )
    spread_some(2)

    wanted = []
    for s in range(spans):
        device, place = jnp.int32(0), jnp.int32(0)
        for g in range(n * spans):
            hit = slots_ref[g] == me * spans + s
            device = jnp.where(hit, g // spans, device)
            place = jnp.where(hit, g % spans, place)
        wanted.append((device, place))

    def relay(p):
        for d in range(1, chips):
            origin = behind(d, core)
            await_piece(p, origin, d)
            remote(p, bufs[p].at[origin], origin, chips, sibling).start()

    def complete(p):
        several(bufs[p], chips - 1, None, recv.at[p, chips]).wait_recv()
        select(p)
        if p < count - 1:
            publish(p)

    def page_copy(p, target, origin, held=False):
        ref = zbufs[p].at[origin]
        return pltpu.make_async_remote_copy(
            src_ref=ref,
            dst_ref=ref,
            send_sem=page_send.at[p],
            recv_sem=page_recv.at[count + p if held else p],
            device_id={"page": target},
            device_id_type=MESH,
        )

    def within(place):
        return jnp.logical_and(place >= 0, place < n_page)

    def handed(p):
        return n_page == 4 and p in HANDED

    inner = jnp.logical_and(page > 0, page < n_page - 1)

    def select(p):
        for s in range(spans):
            device, place = wanted[s]
            for j in range(2):
                zbufs[p][page, j, s] = bufs[p][device, j, place]

    def publish(p):
        if not handed(p):
            for index in range(1, n_page):
                page_copy(p, (page + index) % n_page, page).start()
            return
        for sign in (-1, 1):
            @pl.when(within(page + sign))
            def _(sign=sign):
                page_copy(p, page + sign, page).start()

            @pl.when(within(page + 3 * sign))
            def _(sign=sign):
                page_copy(p, page + 2 * sign, page, True).start()

            @pl.when(jnp.logical_and(within(page + 2 * sign), inner))
            def _(sign=sign):
                page_copy(p, page + 2 * sign, page).start()

    def hand_on(p):
        if handed(p):
            for sign in (-1, 1):
                @pl.when(jnp.logical_and(within(page - 2 * sign), inner))
                def _(sign=sign):
                    page_copy(p, page + sign, page - 2 * sign, True).wait_recv()
                    page_copy(p, page + sign, page - 2 * sign).start()

    def each_amount(p, outer_count, inner_count, action):
        if not handed(p):
            action(n_page - 1)
            return

        @pl.when(inner)
        def _():
            action(inner_count)

        @pl.when(jnp.logical_not(inner))
        def _():
            action(outer_count)

    def foreign(index, owner, target):
        ref = fbuf.at[owner]
        return pltpu.make_async_remote_copy(
            src_ref=ref,
            dst_ref=ref,
            send_sem=far_send.at[0],
            recv_sem=far_recv.at[index],
            device_id={"ctx": target},
            device_id_type=MESH,
        )

    def foreign_spread():
        several(zbufs[count - 1], n_page - 1, None, page_recv.at[count - 1]).wait_recv()
        for d in range(1, chips):
            foreign(d, me, ahead(d)).start()
        foreign(0, me, sibling).start()

    def foreign_relay():
        for d in range(1, chips):
            origin = behind(d, core)
            foreign(d, origin, sibling).wait_recv()
            foreign(chips, origin, sibling).start()

    def foreign_complete():
        foreign(0, sibling, sibling).wait_recv()
        several(fbuf, chips - 1, None, far_recv.at[chips]).wait_recv()
        for s in range(spans):
            device, place = wanted[s]
            for k in range(1, n_page):
                for j in range(2):
                    zbufs[count - 1][(page + k) % n_page, j, s] = fbuf[device, k - 1, j, place]

    for p in range(count):
        mine[p].wait()
        await_piece(p, sibling, 0)

    def beside(j, t):
        return jnp.concatenate([bufs[p][sibling, j, t] for p in range(count)], axis=0)

    def meet(c):
        spread_some(3)
        relay(0)

    attend([Chunk([beside], SPAN, 1, vts[0], False)], idle, idle, meet, False)

    complete(0)
    def rows_of(some, device):
        return lambda j, t: jnp.concatenate([bufs[p][device, j, t] for p in some], axis=0)

    group = [
        Chunk(
            [rows_of(some, device) for device in order[2:]],
            sum(PIECES[p] for p in some), 2, vts[c % 2], False,
        )
        for c, some in enumerate(CHUNKS)
    ]

    def early(c):
        if c == 0:
            foreign_spread()
            relay(1)
        elif c == 1:
            complete(2)
            relay(3)

    def between(c):
        if c == 0:
            complete(1)
            relay(2)
        elif c == 1:
            complete(3)
            hand_on(0)
        else:
            foreign_relay()

    def middle(c):
        if c == 2:
            hand_on(1)

    attend(group, early, middle, between, True)
    foreign_complete()

    finish = pltpu.make_async_copy(att, att_out, out_sem.at[0])
    finish.start()

    for p in range(count - 1):
        each_amount(
            p, 3, 2, lambda k, p=p: several(zbufs[p], k, None, page_recv.at[p]).wait_recv()
        )

    lanes = lax.broadcasted_iota(jnp.int32, (8, DH), 1)
    for s in range(spans):
        for j in range(2):
            levels = jnp.zeros((8, DH), jnp.float32)
            for h in range(n_page):
                level = None
                for p in range(count):
                    high = jnp.max(jnp.abs(zbufs[p][h, j, s].astype(jnp.float32)), axis=0, keepdims=True)
                    level = high if level is None else jnp.maximum(level, high)
                level = jnp.max(level, axis=1, keepdims=True) + 1e-06
                share = 1.0 / level
                for p in range(count):
                    cache[s, h, j, starts[p] : starts[p] + PIECES[p]] = (
                        zbufs[p][h, j, s].astype(jnp.float32) * share
                    ).astype(jnp.bfloat16)
                levels = jnp.where(lanes == h, level, levels)
            scales[s, j] = levels
    last = [
        pltpu.make_async_copy(cache, cache_out, out_sem.at[1]),
        pltpu.make_async_copy(scales, scales_out, out_sem.at[2]),
    ]
    for copy in last:
        copy.start()
    for p in range(count):
        several(bufs[p], n - 1, send.at[p], None).wait_send()
        each_amount(
            p, 2, 4, lambda k, p=p: several(zbufs[p], k, page_send.at[p], None).wait_send()
        )
    several(fbuf, n - 1, far_send.at[0], None).wait_send()
    finish.wait()
    for copy in last:
        copy.wait()


def place_results(att_in, cache_in, scales_in, att_out, cache_out, scales_out, sems):
    parts = sems.shape[0] - cache_in.shape[0]
    rows = att_in.shape[0] // parts
    moves = [
        (att_in.at[pl.ds(j * rows, rows)], att_out.at[pl.ds(j * rows, rows)]) for j in range(parts)
    ]
    moves += [(cache_in.at[s], cache_out.at[s]) for s in range(cache_in.shape[0])]
    moves = [pltpu.make_async_copy(*pair, sems.at[j]) for j, pair in enumerate(moves)]
    for copy in moves:
        copy.start()
    for s in range(scales_out.shape[0]):
        for j in range(scales_out.shape[1]):
            scales_out[s, j : j + 1] = scales_in[s, j, :1, : scales_out.shape[2]]
    for copy in moves:
        copy.wait()


def on_device(n, n_page, queries, keys, values, span_table, page_slots):
    rows = queries.shape[0]
    heads = queries.shape[1] // DH
    spans = rows // SPAN
    units = heads // PAIR * spans
    wide = PAIR * SPAN
    rows_most = max(sum(PIECES[p] for p in some) for some in CHUNKS)
    most = max(spans * SPAN, (n - 2) * spans * rows_most)
    padded = -(-most // 128) * 128
    any_space = pl.BlockSpec(memory_space=pl.ANY)
    vmem = pl.BlockSpec(memory_space=pltpu.VMEM)
    hbm = pl.BlockSpec(memory_space=pltpu.HBM)
    count = len(PIECES)
    results = (
        jax.ShapeDtypeStruct((rows, heads * DH), jnp.bfloat16),
        jax.ShapeDtypeStruct((spans, n_page, 2, PAGE, DH), jnp.bfloat16),
        jax.ShapeDtypeStruct((spans, 2, 8, DH), jnp.float32),
    )
    attended, cache, scales = pl.pallas_call(
        functools.partial(kernel, n, n_page, heads, spans),
        out_shape=results,
        in_specs=[hbm] * 5,
        out_specs=(any_space,) * 3,
        scratch_shapes=[
            pltpu.SMEM(span_table.shape, jnp.int32),
            pltpu.SMEM(page_slots.shape, jnp.int32),
            pltpu.SMEM((spans * n * spans,), jnp.float32),
            pltpu.VMEM(queries.shape, jnp.bfloat16),
            pltpu.VMEM((2, spans, SPAN, DH), jnp.bfloat16),
            [pltpu.VMEM((DH + 16, padded), jnp.bfloat16)] * 2,
            pltpu.VMEM((most, wide), jnp.float32),
            pltpu.VMEM((most, wide), jnp.float32),
            pltpu.VMEM((most, wide), jnp.bfloat16),
            pltpu.VMEM((most, wide), jnp.bfloat16),
            pltpu.VMEM((units, 8, wide), jnp.float32),
            pltpu.VMEM((units, DH + 8, wide), jnp.float32),
            pltpu.VMEM(queries.shape, jnp.bfloat16),
            pltpu.VMEM((spans, n_page, 2, PAGE, DH), jnp.bfloat16),
            pltpu.VMEM((spans, 2, 8, DH), jnp.float32),
            pltpu.SemaphoreType.DMA((count,)),
            pltpu.SemaphoreType.DMA((count, n // 2 + 1)),
            pltpu.SemaphoreType.DMA((5 + count,)),
            pltpu.SemaphoreType.DMA((count,)),
            pltpu.SemaphoreType.DMA((count + len(HANDED),)),
            pltpu.SemaphoreType.DMA((1,)),
            pltpu.SemaphoreType.DMA((n // 2 + 1,)),
            pltpu.SemaphoreType.DMA((3,)),
            pltpu.VMEM((n, n_page - 1, 2, spans, PIECES[-1], DH), jnp.bfloat16),
        ]
        + [pltpu.VMEM((n, 2, spans, p, DH), jnp.bfloat16) for p in PIECES]
        + [pltpu.VMEM((n_page, 2, spans, p, DH), jnp.bfloat16) for p in PIECES],
        compiler_params=pltpu.CompilerParams(
            collective_id=0, has_side_effects=True, vmem_limit_bytes=48 * 2**20
        ),
    )(
        *(
            pltpu.with_memory_space_constraint(x, pltpu.HBM)
            for x in (
                span_table,
                page_slots,
                queries,
                keys.reshape(spans, SPAN, DH),
                values.reshape(spans, SPAN, DH),
            )
        )
    )
    attended, cache, scales = pl.pallas_call(
        place_results,
        out_shape=results[:2] + (jax.ShapeDtypeStruct((spans, 2, n_page), jnp.float32),),
        in_specs=[any_space, any_space, vmem],
        out_specs=(any_space, any_space, vmem),
        scratch_shapes=[
            pltpu.SemaphoreType.DMA((4 + spans,)),
        ],
        compiler_params=pltpu.CompilerParams(vmem_limit_bytes=16 * 2**20),
    )(attended, cache, scales)
    return attended, cache, scales.transpose(0, 2, 1)


def solution(mesh):
    placed = (P("ctx", "page"), P("ctx", "page"), P("ctx", "page"), P(), P())
    return jax.shard_map(
        functools.partial(on_device, mesh.shape["ctx"], mesh.shape["page"]),
        mesh=mesh,
        in_specs=placed,
        out_specs=(P("ctx", "page"), P("ctx", None, None, None, None), P("ctx", None, None)),
        check_vma=False,
    )
```

```python
import functools
import math

import jax
import jax.numpy as jnp
from jax import lax
from jax.experimental import pallas as pl
from jax.experimental.pallas import tpu as pltpu
from jax.sharding import PartitionSpec as P

DH = 128
PAGE = 128
SPAN = 128
HIDE = -1e30
PAIR = 2
PIECES = (32, 32, 32, 32)
CHUNKS = ((0,), (1,), (2, 3))
HANDED = (0, 1)
MESH = pl.DeviceIdType.MESH


def kernel(
    n, n_page, heads, spans, table_in, slots_in, q_in, k_in, v_in,
    att_out, cache_out, scales_out,
    table_ref, slots_ref, bias, q_ref, own, vts, s0, s1, p0, p1,
    tops, acc, att, cache, scales, send, recv, own_sem, page_send, page_recv, far_send, far_recv, fbuf,
    *pieces,
):
    count = len(PIECES)
    bufs, zbufs = pieces[:count], pieces[count:]
    starts = [sum(PIECES[:p]) for p in range(count)]
    chips = n // 2
    pairs = heads // PAIR
    wide = PAIR * SPAN
    units = pairs * spans
    me = lax.axis_index("ctx")
    page = lax.axis_index("page")
    chip = me // 2
    core = me % 2
    sibling = 2 * chip + 1 - core
    rate = DH ** (-0.5) * math.log2(math.e)

    even = chips & (chips - 1) == 0

    def across_from(d, back):
        if not even:
            return (chip + chips - d) % chips if back else (chip + d) % chips
        place, bit = chip, 1
        while bit < chips:
            if d & bit:
                place = place + bit * (1 - 2 * (place // bit % 2))
            bit *= 2
        return place

    def ahead(d):
        return 2 * across_from(d, False) + core

    def behind(d, c):
        return 2 * across_from(d, True) + c

    barrier = pltpu.get_barrier_semaphore()
    for d in range(1, chips):
        pl.semaphore_signal(barrier, inc=1, device_id={"ctx": ahead(d)}, device_id_type=MESH)
    pl.semaphore_signal(barrier, inc=1, device_id={"ctx": sibling}, device_id_type=MESH)
    for d in range(1, n_page):
        pl.semaphore_signal(
            barrier, inc=1, device_id={"page": (page + d) % n_page}, device_id_type=MESH
        )

    local = []

    def fetch(src, dst, j):
        copy = pltpu.make_async_copy(src, dst, own_sem.at[j])
        copy.start()
        local.append(copy)

    fetch(k_in, own.at[0], 0)
    fetch(v_in, own.at[1], 1)
    fetch(table_in, table_ref, 2)
    fetch(q_in, q_ref, 3)
    fetch(slots_in, slots_ref, 4)

    pl.semaphore_wait(barrier, chips + n_page - 1)

    def remote(p, src, owner, index, target):
        return pltpu.make_async_remote_copy(
            src_ref=src,
            dst_ref=bufs[p].at[owner],
            send_sem=send.at[p],
            recv_sem=recv.at[p, index],
            device_id={"ctx": target},
            device_id_type=MESH,
        )

    def several(ref, copies, send_sem, recv_sem):
        some = ref.at[pl.ds(0, copies)]
        return pltpu.make_async_remote_copy(
            src_ref=some,
            dst_ref=some,
            send_sem=recv_sem if send_sem is None else send_sem,
            recv_sem=send_sem if recv_sem is None else recv_sem,
            device_id={"ctx": sibling},
            device_id_type=MESH,
        )

    def await_piece(p, owner, index):
        remote(p, bufs[p].at[owner], owner, index, sibling).wait_recv()

    def piece_of(p):
        return own.at[:, :, pl.ds(starts[p], PIECES[p])]

    def spread(p):
        for d in range(chips - 1, 0, -1):
            remote(p, piece_of(p), me, d, ahead(d)).start()

    def across(index):
        return pltpu.make_async_remote_copy(
            src_ref=piece_of(count - 1),
            dst_ref=fbuf.at[me, n_page - index - 1],
            send_sem=page_send.at[count - 1],
            recv_sem=page_recv.at[count - 1],
            device_id={"page": (page + index) % n_page},
            device_id_type=MESH,
        )

    for copy in local[:2]:
        copy.wait()
    spread(0)
    for index in range(1, n_page):
        across(index).start()
    for p in range(count):
        remote(p, piece_of(p), me, 0, sibling).start()

    rows_at = lax.broadcasted_iota(jnp.int32, (SPAN, wide), 1) % SPAN
    keys_at = lax.broadcasted_iota(jnp.int32, (SPAN, wide), 0)
    for vt in vts:
        vt[DH:, :] = jnp.ones((vt.shape[0] - DH, vt.shape[1]), jnp.bfloat16)
    for copy in local[2:]:
        copy.wait()
    mine = []
    for p in range(count):
        copy = pltpu.make_async_copy(piece_of(p), bufs[p].at[me], own_sem.at[p])
        copy.start()
        mine.append(copy)

    order = [me, sibling]
    for d in range(1, chips):
        order += [behind(d, core), behind(d, 1 - core)]
    for i in range(spans):
        here = table_ref[me * spans + i]
        for d, device in enumerate(order):
            for t in range(spans):
                there = table_ref[device * spans + t]
                bias[(i * n + d) * spans + t] = jnp.where(there < here, 0.0, HIDE)

    class Chunk:
        def __init__(self, parts, rows, base, vt, diagonal):
            self.parts = parts
            self.rows = rows
            self.base = base
            self.vt = vt
            self.diagonal = diagonal
            self.blocks = len(parts) * spans
            self.size = self.blocks * rows

        def stage(self):
            other = [part(1, t) for part in self.parts for t in range(spans)]
            self.vt[:DH, : self.size] = jnp.concatenate(other, axis=0).T

        def keys(self):
            return jnp.concatenate(
                [part(0, t) for part in self.parts for t in range(spans)], axis=0
            )

        def shift(self, i, t):
            if self.diagonal and t == i:
                return None
            return bias[i * n * spans + self.base * spans + t]

    def pair_of(u, i):
        return (u - i) // spans if isinstance(u, int) else lax.div(u - i, spans)

    def score(chunk, u, i, s):
        g = pair_of(u, i)
        keys = chunk.keys()
        value = jnp.concatenate(
            [
                lax.dot_general(
                    keys,
                    q_ref[
                        pl.ds(i * SPAN, SPAN),
                        pl.ds(pl.multiple_of((g * PAIR + h) * DH, DH), DH),
                    ],
                    (((1,), (1,)), ((), ())),
                    preferred_element_type=jnp.float32,
                )
                for h in range(PAIR)
            ],
            axis=1,
        )
        best = None
        rows = chunk.rows
        for t in range(chunk.blocks):
            part = value[t * rows : (t + 1) * rows]
            offset = chunk.shift(i, t)
            if offset is None:
                part = jnp.where(keys_at > rows_at, HIDE, part)
            s[t * rows : (t + 1) * rows] = part
            high = part[:8]
            for r in range(1, rows // 8):
                high = jnp.maximum(high, part[r * 8 : (r + 1) * 8])
            if offset is not None:
                high = high + offset
            best = high if best is None else jnp.maximum(best, high)
        best = jnp.broadcast_to(jnp.max(best, axis=0, keepdims=True), (8, wide))
        if chunk.diagonal:
            tops[u] = best
            return best, best
        old = tops[u]
        new = jnp.maximum(old, best)
        tops[u] = new
        return new, jnp.exp2((old - new) * rate)

    def weigh(chunk, i, high, s, w):
        rows = chunk.rows
        for t in range(chunk.blocks):
            offset = chunk.shift(i, t)
            level = high if offset is None else high - offset
            level = jnp.concatenate([level] * (rows // 8), axis=0)
            w[t * rows : (t + 1) * rows] = jnp.exp2(
                (s[t * rows : (t + 1) * rows] - level) * rate
            ).astype(jnp.bfloat16)

    def gather(chunk, u, factor, w):
        update = jnp.dot(
            chunk.vt[:, : chunk.size], w[: chunk.size], preferred_element_type=jnp.float32
        )
        update = update[: DH + 8]
        if not chunk.diagonal:
            update = acc[u] * jnp.concatenate([factor] * (DH // 8 + 1), axis=0) + update
        acc[u] = update
        return update

    def finish_unit(u, i, value):
        g = pair_of(u, i)
        share = 1.0 / value[DH : DH + 8]
        value = (value[:DH] * jnp.concatenate([share] * (DH // 8), axis=0)).T
        for h in range(PAIR):
            att[
                pl.ds(i * SPAN, SPAN), pl.ds(pl.multiple_of((g * PAIR + h) * DH, DH), DH)
            ] = value[h * SPAN : (h + 1) * SPAN].astype(jnp.bfloat16)

    ss, ww = (s0, s1), (p0, p1)

    def steps_of(chunk):
        most = min(pairs // 2, max(1, 8 * 512 // (spans * chunk.size)))
        return max(k for k in range(1, most + 1) if pairs % k == 0) * spans

    def attend(group, early, middle, between, final):
        pers = [steps_of(chunk) for chunk in group]

        def turn(j, carry, c, head, tail):
            chunk, per = group[c], pers[c]
            (high, factor), late = carry
            for x in range(per):
                u = per * j + x
                now = x % 2
                weigh(chunk, x % spans, high, ss[now], ww[now])
                if x < per - 1 or not tail:
                    after = score(chunk, u + 1, (x + 1) % spans, ss[1 - now])
                elif c + 1 < len(group):
                    after = score(group[c + 1], 0, 0, ss[1 - now])
                else:
                    after = (high, factor)
                if x or not head:
                    value = gather(chunk, u - 1, late, ww[1 - now])
                    if x and final and c == len(group) - 1:
                        finish_unit(u - 1, (x - 1) % spans, value)
                elif c:
                    gather(group[c - 1], units - 1, late, ww[1 - now])
                late = factor
                high, factor = after
            return (high, factor), late

        group[0].stage()
        start = score(group[0], 0, 0, s0)
        carry = start, start[1]
        for c in range(len(group)):
            turns = units // pers[c]
            early(c)
            if turns > 1:
                carry = turn(0, carry, c, True, False)
                half = turns // 2
                for part, (low, high) in enumerate(((1, half), (half, turns - 1))):
                    if part:
                        middle(c)
                    if low < high:
                        carry = lax.fori_loop(
                            low,
                            high,
                            lambda j, carry, c=c: turn(j, carry, c, False, False),
                            carry,
                        )
            else:
                middle(c)
            between(c)
            if c + 1 < len(group):
                group[c + 1].stage()
            carry = turn(turns - 1, carry, c, turns == 1, True)
        per = pers[-1]
        value = gather(group[-1], units - 1, carry[1], ww[(per - 1) % 2])
        if final:
            finish_unit(units - 1, spans - 1, value)

            for j in range(units // per - 1):
                u = per * j + per - 1
                finish_unit(u, spans - 1, acc[u])

    def idle(c):
        pass

    def spread_some(k):
        for p in range(1, count):
            if min(p, 3) == k:
                spread(p)

    attend(
        [Chunk([lambda j, t: own[j, t]], SPAN, 0, vts[0], True)],
        idle, idle, lambda c: spread_some(1), False,
    )
    spread_some(2)

    wanted = []
    for s in range(spans):
        device, place = jnp.int32(0), jnp.int32(0)
        for g in range(n * spans):
            hit = slots_ref[g] == me * spans + s
            device = jnp.where(hit, g // spans, device)
            place = jnp.where(hit, g % spans, place)
        wanted.append((device, place))

    def relay(p):
        for d in range(1, chips):
            origin = behind(d, core)
            await_piece(p, origin, d)
            remote(p, bufs[p].at[origin], origin, chips, sibling).start()

    def complete(p):
        several(bufs[p], chips - 1, None, recv.at[p, chips]).wait_recv()
        select(p)
        if p < count - 1:
            publish(p)

    def page_copy(p, target, origin, held=False):
        ref = zbufs[p].at[origin]
        return pltpu.make_async_remote_copy(
            src_ref=ref,
            dst_ref=ref,
            send_sem=page_send.at[p],
            recv_sem=page_recv.at[count + p if held else p],
            device_id={"page": target},
            device_id_type=MESH,
        )

    def within(place):
        return jnp.logical_and(place >= 0, place < n_page)

    def handed(p):
        return n_page == 4 and p in HANDED

    inner = jnp.logical_and(page > 0, page < n_page - 1)

    def select(p):
        for s in range(spans):
            device, place = wanted[s]
            for j in range(2):
                zbufs[p][page, j, s] = bufs[p][device, j, place]

    def publish(p):
        if not handed(p):
            for index in range(1, n_page):
                page_copy(p, (page + index) % n_page, page).start()
            return
        for sign in (-1, 1):
            @pl.when(within(page + sign))
            def _(sign=sign):
                page_copy(p, page + sign, page).start()

            @pl.when(within(page + 3 * sign))
            def _(sign=sign):
                page_copy(p, page + 2 * sign, page, True).start()

            @pl.when(jnp.logical_and(within(page + 2 * sign), inner))
            def _(sign=sign):
                page_copy(p, page + 2 * sign, page).start()

    def hand_on(p):
        if handed(p):
            for sign in (-1, 1):
                @pl.when(jnp.logical_and(within(page - 2 * sign), inner))
                def _(sign=sign):
                    page_copy(p, page + sign, page - 2 * sign, True).wait_recv()
                    page_copy(p, page + sign, page - 2 * sign).start()

    def each_amount(p, outer_count, inner_count, action):
        if not handed(p):
            action(n_page - 1)
            return

        @pl.when(inner)
        def _():
            action(inner_count)

        @pl.when(jnp.logical_not(inner))
        def _():
            action(outer_count)

    def foreign(index, owner, target):
        ref = fbuf.at[owner]
        return pltpu.make_async_remote_copy(
            src_ref=ref,
            dst_ref=ref,
            send_sem=far_send.at[0],
            recv_sem=far_recv.at[index],
            device_id={"ctx": target},
            device_id_type=MESH,
        )

    def foreign_spread():
        several(zbufs[count - 1], n_page - 1, None, page_recv.at[count - 1]).wait_recv()
        for d in range(chips - 1, 0, -1):
            foreign(d, me, ahead(d)).start()
        foreign(0, me, sibling).start()

    def foreign_relay():
        for d in range(1, chips):
            origin = behind(d, core)
            foreign(d, origin, sibling).wait_recv()
            foreign(chips, origin, sibling).start()

    def foreign_complete():
        foreign(0, sibling, sibling).wait_recv()
        several(fbuf, chips - 1, None, far_recv.at[chips]).wait_recv()
        for s in range(spans):
            device, place = wanted[s]
            for k in range(1, n_page):
                for j in range(2):
                    zbufs[count - 1][(page + k) % n_page, j, s] = fbuf[device, k - 1, j, place]

    for p in range(count):
        mine[p].wait()
        await_piece(p, sibling, 0)

    def beside(j, t):
        return jnp.concatenate([bufs[p][sibling, j, t] for p in range(count)], axis=0)

    def meet(c):
        spread_some(3)
        relay(0)

    attend([Chunk([beside], SPAN, 1, vts[0], False)], idle, idle, meet, False)

    complete(0)
    def rows_of(some, device):
        return lambda j, t: jnp.concatenate([bufs[p][device, j, t] for p in some], axis=0)

    group = [
        Chunk(
            [rows_of(some, device) for device in order[2:]],
            sum(PIECES[p] for p in some), 2, vts[c % 2], False,
        )
        for c, some in enumerate(CHUNKS)
    ]

    def early(c):
        if c == 0:
            foreign_spread()
            relay(1)
        elif c == 1:
            complete(2)
            relay(3)

    def between(c):
        if c == 0:
            complete(1)
            relay(2)
        elif c == 1:
            complete(3)
            hand_on(0)
        else:
            foreign_relay()

    def middle(c):
        if c == 2:
            hand_on(1)

    attend(group, early, middle, between, True)
    foreign_complete()

    finish = pltpu.make_async_copy(att, att_out, own_sem.at[0])
    finish.start()

    for p in range(count - 1):
        each_amount(
            p, 3, 2, lambda k, p=p: several(zbufs[p], k, None, page_recv.at[p]).wait_recv()
        )

    lanes = lax.broadcasted_iota(jnp.int32, (8, DH), 1)
    for s in range(spans):
        for j in range(2):
            levels = jnp.zeros((8, DH), jnp.float32)
            for h in range(n_page):
                level = None
                for p in range(count):
                    high = jnp.max(jnp.abs(zbufs[p][h, j, s].astype(jnp.float32)), axis=0, keepdims=True)
                    level = high if level is None else jnp.maximum(level, high)
                level = jnp.max(level, axis=1, keepdims=True) + 1e-06
                share = 1.0 / level
                for p in range(count):
                    cache[s, h, j, starts[p] : starts[p] + PIECES[p]] = (
                        zbufs[p][h, j, s].astype(jnp.float32) * share
                    ).astype(jnp.bfloat16)
                levels = jnp.where(lanes == h, level, levels)
            scales[s, j] = levels
    last = [
        pltpu.make_async_copy(cache, cache_out, own_sem.at[1]),
        pltpu.make_async_copy(scales, scales_out, own_sem.at[2]),
    ]
    for copy in last:
        copy.start()
    for p in range(count):
        several(bufs[p], n - 1, send.at[p], None).wait_send()
        each_amount(
            p, 2, 4, lambda k, p=p: several(zbufs[p], k, page_send.at[p], None).wait_send()
        )
    several(fbuf, n - 1, far_send.at[0], None).wait_send()
    finish.wait()
    for copy in last:
        copy.wait()


def place_results(att_in, cache_in, scales_in, att_out, cache_out, scales_out, sems):
    parts = sems.shape[0] - cache_in.shape[0]
    rows = att_in.shape[0] // parts
    moves = [
        (att_in.at[pl.ds(j * rows, rows)], att_out.at[pl.ds(j * rows, rows)]) for j in range(parts)
    ]
    moves += [(cache_in.at[s], cache_out.at[s]) for s in range(cache_in.shape[0])]
    moves = [pltpu.make_async_copy(*pair, sems.at[j]) for j, pair in enumerate(moves)]
    for copy in moves:
        copy.start()
    for s in range(scales_out.shape[0]):
        for j in range(scales_out.shape[1]):
            scales_out[s, j : j + 1] = scales_in[s, j, :1, : scales_out.shape[2]]
    for copy in moves:
        copy.wait()


def on_device(n, n_page, queries, keys, values, span_table, page_slots):
    rows = queries.shape[0]
    heads = queries.shape[1] // DH
    spans = rows // SPAN
    units = heads // PAIR * spans
    wide = PAIR * SPAN
    rows_most = max(sum(PIECES[p] for p in some) for some in CHUNKS)
    most = max(spans * SPAN, (n - 2) * spans * rows_most)
    padded = -(-most // 128) * 128
    any_space = pl.BlockSpec(memory_space=pl.ANY)
    vmem = pl.BlockSpec(memory_space=pltpu.VMEM)
    hbm = pl.BlockSpec(memory_space=pltpu.HBM)
    count = len(PIECES)
    results = (
        jax.ShapeDtypeStruct((rows, heads * DH), jnp.bfloat16),
        jax.ShapeDtypeStruct((spans, n_page, 2, PAGE, DH), jnp.bfloat16),
        jax.ShapeDtypeStruct((spans, 2, 8, DH), jnp.float32),
    )
    attended, cache, scales = pl.pallas_call(
        functools.partial(kernel, n, n_page, heads, spans),
        out_shape=results,
        in_specs=[hbm] * 5,
        out_specs=(any_space,) * 3,
        scratch_shapes=[
            pltpu.SMEM(span_table.shape, jnp.int32),
            pltpu.SMEM(page_slots.shape, jnp.int32),
            pltpu.SMEM((spans * n * spans,), jnp.float32),
            pltpu.VMEM(queries.shape, jnp.bfloat16),
            pltpu.VMEM((2, spans, SPAN, DH), jnp.bfloat16),
            [pltpu.VMEM((DH + 16, padded), jnp.bfloat16)] * 2,
            pltpu.VMEM((most, wide), jnp.float32),
            pltpu.VMEM((most, wide), jnp.float32),
            pltpu.VMEM((most, wide), jnp.bfloat16),
            pltpu.VMEM((most, wide), jnp.bfloat16),
            pltpu.VMEM((units, 8, wide), jnp.float32),
            pltpu.VMEM((units, DH + 8, wide), jnp.float32),
            pltpu.VMEM(queries.shape, jnp.bfloat16),
            pltpu.VMEM((spans, n_page, 2, PAGE, DH), jnp.bfloat16),
            pltpu.VMEM((spans, 2, 8, DH), jnp.float32),
            pltpu.SemaphoreType.DMA((count,)),
            pltpu.SemaphoreType.DMA((count, n // 2 + 1)),
            pltpu.SemaphoreType.DMA((max(5, count),)),
            pltpu.SemaphoreType.DMA((count,)),
            pltpu.SemaphoreType.DMA((count + len(HANDED),)),
            pltpu.SemaphoreType.DMA((1,)),
            pltpu.SemaphoreType.DMA((n // 2 + 1,)),
            pltpu.VMEM((n, n_page - 1, 2, spans, PIECES[-1], DH), jnp.bfloat16),
        ]
        + [pltpu.VMEM((n, 2, spans, p, DH), jnp.bfloat16) for p in PIECES]
        + [pltpu.VMEM((n_page, 2, spans, p, DH), jnp.bfloat16) for p in PIECES],
        compiler_params=pltpu.CompilerParams(
            collective_id=0, has_side_effects=True, vmem_limit_bytes=48 * 2**20
        ),
    )(
        *(
            pltpu.with_memory_space_constraint(x, pltpu.HBM)
            for x in (
                span_table,
                page_slots,
                queries,
                keys.reshape(spans, SPAN, DH),
                values.reshape(spans, SPAN, DH),
            )
        )
    )
    attended, cache, scales = pl.pallas_call(
        place_results,
        out_shape=results[:2] + (jax.ShapeDtypeStruct((spans, 2, n_page), jnp.float32),),
        in_specs=[any_space, any_space, vmem],
        out_specs=(any_space, any_space, vmem),
        scratch_shapes=[
            pltpu.SemaphoreType.DMA((4 + spans,)),
        ],
        compiler_params=pltpu.CompilerParams(vmem_limit_bytes=16 * 2**20),
    )(attended, cache, scales)
    return attended, cache, scales.transpose(0, 2, 1)


def solution(mesh):
    placed = (P("ctx", "page"), P("ctx", "page"), P("ctx", "page"), P(), P())
    return jax.shard_map(
        functools.partial(on_device, mesh.shape["ctx"], mesh.shape["page"]),
        mesh=mesh,
        in_specs=placed,
        out_specs=(P("ctx", "page"), P("ctx", None, None, None, None), P("ctx", None, None)),
        check_vma=False,
    )
```
